512 devices in a mesh: ctx: 64 (over z_lo, x, y), head: 8 (over z_hi, core).
Axes of the slice: x: 4, y: 8, z: 8 (z_hi: 4, z_lo: 2; z = z_hi * 2 + z_lo), core: 2. Of those that a mesh axis runs over, the one named last changes fastest.
Arguments:
- queries: bfloat16 [10240, 8192], P(('ctx', 'head')), may hold values from -18 to 18
- keys: bfloat16 [10240, 1024], P(('ctx', 'head')), may hold values from -4.5 to 4.5
- values: bfloat16 [10240, 1024], P(('ctx', 'head')), may hold values from -12 to 12
- block_order: int32 [128], replicated, may hold values from 0 to 127, each once
Outputs:
- attended: bfloat16 [10240, 8192], P(('ctx', 'head'))
The draws below stay inside these ranges and needn't reach their ends.
Inputs may be any that keep to these rules, and one draw needn't show every extreme that they name: Storage block b holds sequence block block_order[b], its tokens in order; block_order is a permutation.
All inputs are finite; a program needn't handle non-finite values.
Results may differ from the reference program's by a relative error of at most 0.0049.
Values may be sent and summed in bfloat16 or wider, within the bound.
No kernel may reach another device: no remote copies, remote signals or barrier semaphores. Data moves between devices by JAX's collectives and lax.ppermute only.
A program may use at most 64 MiB of HBM per device.

```python
import jax
import jax.numpy as jnp
from jax import lax

QUERY_HEADS = 64
VALUE_KEY_HEADS = 8
HEAD_DIMENSION = 128
BLOCK_TOKENS = 80
SEQUENCE_TOKENS = 10240
NBLK = 128


def key_base(key):
    key_start_offset = jax.random.fold_in(key, 7)
    return jnp.clip(jax.random.normal(key_start_offset, (SEQUENCE_TOKENS, VALUE_KEY_HEADS, HEAD_DIMENSION), jnp.float32), -4.0, 4.0)


def draw_keys(key, part):
    lookup_rows = key_base(key)
    return lookup_rows.reshape(SEQUENCE_TOKENS, VALUE_KEY_HEADS * HEAD_DIMENSION).astype(jnp.bfloat16)


def draw_queries(key, part):
    query_key = jax.random.fold_in(key, 23)
    start_offset = 2.0 * jnp.clip(jax.random.normal(query_key, (SEQUENCE_TOKENS, QUERY_HEADS, HEAD_DIMENSION), jnp.float32), -5.0, 5.0)
    return start_offset.reshape(SEQUENCE_TOKENS, QUERY_HEADS * HEAD_DIMENSION).astype(jnp.bfloat16)


def block_scale(stream_key, dims, shards, smallest, top_value):
    def one(dim, shards_of):
        draws = jax.random.uniform(jax.random.fold_in(jax.random.fold_in(stream_key, 6), dim), (shards_of,), jnp.float32, smallest / len(shards), top_value / len(shards))
        return jnp.repeat(jnp.exp(draws), dims[dim] // shards_of).reshape((-1,) + (1,) * (len(dims) - dim - 1))

    factor_of = one(*shards[0])
    for cut in shards[1:]:
        factor_of = factor_of * one(*cut)
    return factor_of


def noise(key, extent, deviation, reach, cuts=(), kind=jnp.bfloat16):
    drawn = jax.random.normal(key, extent, jnp.float32) * deviation
    if len(cuts) > 0:
        drawn = block_scale(key, extent, cuts, -0.22, 0.18) * drawn
    return jnp.clip(drawn, min=-reach, max=reach).astype(kind)


def setup_inputs(seed: int = 0) -> dict:
    key_list = jax.random.split(jax.random.key(seed), 5)
    return {
        "queries": draw_queries(jax.random.fold_in(key_list[4], 71), 0),
        "keys": draw_keys(jax.random.fold_in(key_list[4], 71), 0),
        "values": noise(key_list[2], (SEQUENCE_TOKENS, VALUE_KEY_HEADS * HEAD_DIMENSION), 3.0, 12.0, ((0, 512),)),
        "block_order": jax.random.permutation(key_list[3], NBLK).astype(jnp.int32),
    }


def reference(queries, keys, values, block_order):
    row_ids = jnp.arange(SEQUENCE_TOKENS, dtype=jnp.int32)
    token_pos = block_order[row_ids // BLOCK_TOKENS] * BLOCK_TOKENS + row_ids % BLOCK_TOKENS
    heads_per_group = QUERY_HEADS // VALUE_KEY_HEADS
    score_scale = HEAD_DIMENSION ** -0.5
    key_lookup_rows = keys.reshape(SEQUENCE_TOKENS, VALUE_KEY_HEADS, HEAD_DIMENSION).astype(jnp.float32)
    value_lookup_rows = values.reshape(SEQUENCE_TOKENS, VALUE_KEY_HEADS, HEAD_DIMENSION).astype(jnp.float32)
    query_block_list = queries.reshape(SEQUENCE_TOKENS // BLOCK_TOKENS, BLOCK_TOKENS, VALUE_KEY_HEADS, heads_per_group, HEAD_DIMENSION)
    pos_blocks = token_pos.reshape(SEQUENCE_TOKENS // BLOCK_TOKENS, BLOCK_TOKENS)

    def one_block(block_item):
        query_block, query_pos = block_item
        scores = jnp.einsum("qkgd,nkd->kgqn", query_block.astype(jnp.float32), key_lookup_rows) * score_scale
        visible = token_pos[None, :] <= query_pos[:, None]
        scores = jnp.where(visible[None, None], scores, -jnp.inf)
        row_max = jnp.max(scores, axis=3, keepdims=True)
        raw_weights = jnp.exp(scores - row_max)
        denominator = jnp.sum(raw_weights, axis=3)
        weights = lax.optimization_barrier(raw_weights.astype(jnp.bfloat16)).astype(jnp.float32)
        numerator = jnp.einsum("kgqn,nkd->qkgd", weights, value_lookup_rows)
        return (numerator / jnp.transpose(denominator, (2, 0, 1))[..., None]).astype(jnp.bfloat16)

    attended = lax.map(one_block, (query_block_list, pos_blocks))
    return attended.reshape(SEQUENCE_TOKENS, QUERY_HEADS * HEAD_DIMENSION)
```

```python
import jax
import jax.numpy as jnp
from jax import lax
from jax.experimental import pallas as pl
from jax.experimental.pallas import tpu as pltpu
from jax.sharding import Mesh, PartitionSpec as P

HEAD_DIMENSION = 128
GROUP_HEADS = 8
PIECE = 20
BLOCK_TOKENS = 80
NX, NY, NZL, NZH = 4, 8, 2, 4
NZ = NZL * NZH
AXES = ("zl", "x", "y", "zh", "core")
LOG2E = 1.4426950408889634
SCALE = HEAD_DIMENSION ** (-0.5) * LOG2E
HIDDEN = -1e30
KEYS = 2 * NY * NZ * PIECE
HALF = KEYS // 2
TOKENS = NZ * PIECE
WIDTH = GROUP_HEADS * HEAD_DIMENSION
ROWS = GROUP_HEADS * BLOCK_TOKENS
TILE = 320


def offsets(index):
    inner = index % 40
    return (inner // 20) * 40 + inner % 20


def attend_kernel(shift, meta, q_ref, own_ref, other_ref, out_ref, qa, ka, va):
    group = pl.program_id(0)
    x_index = meta[0]
    y_index = meta[1]
    core = meta[2]
    query_x = lax.rem(x_index + (NX - shift), NX)

    def block_of(zl, x, y, half):
        return meta[8 + ((zl * NX + x) * NY + y) * 2 + half]

    @pl.when(group == 0)
    def _():
        ka[0:HALF, 0:128] = own_ref[:, 0:128]
        ka[HALF:KEYS, 0:128] = other_ref[:, 0:128]
        va[0:HALF, 0:128] = own_ref[:, 128:256]
        va[HALF:KEYS, 0:128] = other_ref[:, 128:256]
        va[:, 128:256] = jnp.ones((KEYS, 128), jnp.bfloat16)
        token = lax.broadcasted_iota(jnp.int32, (BLOCK_TOKENS, 128), 0)
        lane = lax.broadcasted_iota(jnp.int32, (BLOCK_TOKENS, 128), 1)
        pick = jnp.where(token == lane, 1.0, 0.0).astype(jnp.bfloat16)
        for head in range(GROUP_HEADS):
            qa[head * BLOCK_TOKENS : (head + 1) * BLOCK_TOKENS, 128:256] = pick

    lane = lax.broadcasted_iota(jnp.int32, (BLOCK_TOKENS, 128), 1)
    row = lax.broadcasted_iota(jnp.int32, (BLOCK_TOKENS, 128), 0)
    query_pos = (
        jnp.where(
            lane < 40,
            block_of(group, query_x, y_index, 0),
            block_of(group, query_x, y_index, 1),
        )
        * BLOCK_TOKENS
        + offsets(lane)
        + core * PIECE
    )
    row_offset = offsets(row)
    for side in range(2):
        key_core = core if side == 0 else 1 - core
        gap = query_pos - (row_offset + key_core * PIECE)
        for y in range(NY):
            for zl in range(NZL):
                base = (
                    jnp.where(row < 40, block_of(zl, x_index, y, 0), block_of(zl, x_index, y, 1))
                    * BLOCK_TOKENS
                )
                start = side * HALF + (y * NZL + zl) * BLOCK_TOKENS
                ka[start : start + BLOCK_TOKENS, 128:256] = jnp.where(
                    base > gap, HIDDEN, 0.0
                ).astype(jnp.bfloat16)
    for head in range(GROUP_HEADS):
        qa[head * BLOCK_TOKENS : (head + 1) * BLOCK_TOKENS, 0:128] = q_ref[
            :, head * 128 : (head + 1) * 128
        ]

    stats = jnp.zeros((BLOCK_TOKENS, 128), jnp.float32)
    for tile in range(ROWS // TILE):
        scores = lax.dot_general(
            qa[tile * TILE : (tile + 1) * TILE, :],
            ka[...],
            (((1,), (1,)), ((), ())),
            preferred_element_type=jnp.float32,
        )
        top = jnp.max(scores, axis=1, keepdims=True) * SCALE
        weights = jnp.exp2(scores * SCALE - top).astype(jnp.bfloat16)
        mixed = jnp.dot(weights, va[...], preferred_element_type=jnp.float32)
        total = mixed[:, 128:256]
        result = mixed[:, 0:128] / total
        spread = top + jnp.log2(total)
        for part in range(TILE // BLOCK_TOKENS):
            head = tile * (TILE // BLOCK_TOKENS) + part
            rows = slice(part * BLOCK_TOKENS, (part + 1) * BLOCK_TOKENS)
            out_ref[:, head * 128 : (head + 1) * 128] = result[rows].astype(jnp.bfloat16)
            level = spread[rows]
            high = level.astype(jnp.bfloat16).astype(jnp.float32)
            rest = level - high
            middle = rest.astype(jnp.bfloat16).astype(jnp.float32)
            low = rest - middle
            stats = jnp.where(lane == head, high, stats)
            stats = jnp.where(lane == 8 + head, middle, stats)
            stats = jnp.where(lane == 16 + head, low, stats)
    out_ref[:, WIDTH : WIDTH + 128] = stats.astype(jnp.bfloat16)


def attend(shift, meta, q, own, other):
    def kernel(*refs):
        attend_kernel(shift, *refs)

    return pl.pallas_call(
        kernel,
        out_shape=jax.ShapeDtypeStruct((TOKENS, WIDTH + 128), jnp.bfloat16),
        grid_spec=pltpu.PrefetchScalarGridSpec(
            num_scalar_prefetch=1,
            grid=(TOKENS // BLOCK_TOKENS,),
            in_specs=[
                pl.BlockSpec((BLOCK_TOKENS, WIDTH), lambda g, m: (g, 0)),
                pl.BlockSpec((HALF, 256), lambda g, m: (0, 0)),
                pl.BlockSpec((HALF, 256), lambda g, m: (0, 0)),
            ],
            out_specs=pl.BlockSpec((BLOCK_TOKENS, WIDTH + 128), lambda g, m: (g, 0)),
            scratch_shapes=[
                pltpu.VMEM((ROWS, 256), jnp.bfloat16),
                pltpu.VMEM((KEYS, 256), jnp.bfloat16),
                pltpu.VMEM((KEYS, 256), jnp.bfloat16),
            ],
        ),
        compiler_params=pltpu.CompilerParams(
            dimension_semantics=("arbitrary",), vmem_limit_bytes=48 * 1024 * 1024
        ),
        name=f"attend{shift}",
    )(meta, q, own, other)


def merge_kernel(*refs):
    parts, out_ref = refs[:NX], refs[NX]
    stats = [part[:, WIDTH : WIDTH + 128].astype(jnp.float32) for part in parts]
    for head in range(GROUP_HEADS):
        levels = [
            (s[:, head : head + 1] + s[:, 8 + head : 9 + head]) + s[:, 16 + head : 17 + head]
            for s in stats
        ]
        top = levels[0]
        for level in levels[1:]:
            top = jnp.maximum(top, level)
        shares = [jnp.exp2(level - top) for level in levels]
        total = shares[0]
        for share in shares[1:]:
            total = total + share
        columns = slice(head * 128, (head + 1) * 128)
        mixed = sum(
            part[:, columns].astype(jnp.float32) * share for part, share in zip(parts, shares)
        )
        out_ref[:, columns] = (mixed / total).astype(jnp.bfloat16)


def merge(parts):
    return pl.pallas_call(
        merge_kernel,
        out_shape=jax.ShapeDtypeStruct((TOKENS, WIDTH), jnp.bfloat16),
        name="merge",
    )(*parts)


def ring(shift, size):
    return [(i, (i + shift) % size) for i in range(size)]


def on_device(queries, keys, values, block_order):
    z_axes = ("zl", "zh")
    meta = jnp.concatenate(
        [
            jnp.stack([lax.axis_index("x"), lax.axis_index("y"), lax.axis_index("core")]),
            jnp.zeros((5,), jnp.int32),
            block_order,
        ]
    )
    packed = jnp.concatenate(
        [
            queries.reshape(PIECE, NZ, WIDTH),
            keys.reshape(PIECE, NZ, HEAD_DIMENSION),
            values.reshape(PIECE, NZ, HEAD_DIMENSION),
        ],
        axis=2,
    ).transpose(1, 0, 2)
    packed = lax.all_to_all(packed, z_axes, split_axis=0, concat_axis=0, tiled=True)
    packed = packed.reshape(TOKENS, WIDTH + 256)
    q_own = packed[:, :WIDTH]
    kv = packed[:, WIDTH:]
    q_from = {0: q_own}
    for shift in (2, 1, 3):
        q_from[shift] = lax.ppermute(q_own, "x", ring(shift, NX))
    own = lax.all_to_all(
        jnp.broadcast_to(kv[None], (NY, TOKENS, 256)), "y", split_axis=0, concat_axis=0, tiled=True
    ).reshape(HALF, 256)
    other = lax.ppermute(own, "core", ring(1, 2))
    parts = []
    for shift in (2, 1, 3):
        part = attend(shift, meta, q_from[shift], own, other)
        parts.append(lax.ppermute(part, "x", ring(-shift, NX)))
    parts.append(attend(0, meta, q_own, own, other))
    attended = merge(parts).reshape(NZ, PIECE, WIDTH)
    attended = lax.all_to_all(attended, z_axes, split_axis=0, concat_axis=0, tiled=True)
    return attended.transpose(1, 0, 2).reshape(PIECE, NZ * WIDTH)


def solution(mesh):
    fine = Mesh(mesh.devices.reshape(NZL, NX, NY, NZH, 2), AXES)
    rows = P(AXES, None)
    return jax.shard_map(
        on_device, mesh=fine, in_specs=(rows, rows, rows, P()), out_specs=rows, check_vma=False
    )
```

```python
import jax
import jax.numpy as jnp
from jax import lax
from jax.experimental import pallas as pl
from jax.experimental.pallas import tpu as pltpu
from jax.sharding import Mesh, PartitionSpec as P

HEAD_DIMENSION = 128
GROUP_HEADS = 8
PIECE = 20
BLOCK_TOKENS = 80
NX, NY, NZL, NZH = 4, 8, 2, 4
NZ = NZL * NZH
AXES = ("zl", "x", "y", "zh", "core")
LOG2E = 1.4426950408889634
SCALE = HEAD_DIMENSION ** (-0.5) * LOG2E
HIDDEN = -1e30
NB = NZL * NY * 2
KEYS = NB * BLOCK_TOKENS
TOKENS = NZ * PIECE
WIDTH = GROUP_HEADS * HEAD_DIMENSION
PART = 2 * PIECE
TILES = NX * NZL * 2
ROWS = GROUP_HEADS * PART
CHUNK = 512


def attend_kernel(meta, q_ref, own_ref, other_ref, out_ref, qa, ka, va, kp, qp, sc, mx, tb, acc):
    core = meta[0]

    def load_block(block, carry):
        rank = meta[8 + block]
        both = jnp.concatenate(
            [own_ref[block].astype(jnp.float32), other_ref[block].astype(jnp.float32)], axis=0
        ).astype(jnp.bfloat16)
        start = pl.multiple_of(rank * BLOCK_TOKENS, 16)
        ka[pl.ds(start, BLOCK_TOKENS), :] = both[:, 0:128]
        va[pl.ds(start, BLOCK_TOKENS), 0:128] = both[:, 128:256]
        return carry

    lax.fori_loop(0, NB, load_block, 0, unroll=4)
    va[:, 128:256] = jnp.ones((KEYS, 128), jnp.bfloat16)
    column = lax.broadcasted_iota(jnp.int32, (8, KEYS), 1)
    rank_of = column // BLOCK_TOKENS
    inner = column % BLOCK_TOKENS
    side = inner // PART
    inner = inner % PART
    key_core = jnp.where(side == 0, core, 1 - core)
    key_pos = (inner // PIECE) * PART + inner % PIECE + key_core * PIECE
    base = jnp.zeros((8, KEYS), jnp.int32)
    for rank in range(NB):
        base = jnp.where(rank_of == rank, meta[40 + rank], base)
    kp[...] = base * BLOCK_TOKENS + key_pos

    row = lax.broadcasted_iota(jnp.int32, (PART, 128), 0)
    row_offset = (row // PIECE) * PART + row % PIECE + core * PIECE
    lane = lax.broadcasted_iota(jnp.int32, (PART, 128), 1)
    hidden_row = jnp.full((ROWS, 128), -3e38, jnp.float32)

    def open_tile(tile):
        heads = [
            q_ref[tile, :, head * 128 : (head + 1) * 128].astype(jnp.float32)
            for head in range(GROUP_HEADS)
        ]
        qa[...] = jnp.concatenate(heads, axis=0).astype(jnp.bfloat16)
        pos = row_offset + meta[72 + tile] * BLOCK_TOKENS
        qp[...] = jnp.concatenate([pos] * GROUP_HEADS, axis=0)
        mx[...] = hidden_row

    def score(slot, j):
        start = pl.multiple_of(j * CHUNK, CHUNK)
        s = lax.dot_general(
            qa[...],
            ka[pl.ds(start, CHUNK), :],
            (((1,), (1,)), ((), ())),
            preferred_element_type=jnp.float32,
        )
        top = mx[...]
        own_pos = qp[...]
        for part in range(CHUNK // 128):
            at = pl.multiple_of(start + part * 128, 128)
            seen = kp[0:1, pl.ds(at, 128)] <= own_pos
            piece = jnp.where(seen, s[:, part * 128 : (part + 1) * 128], HIDDEN)
            sc[slot, j, :, part * 128 : (part + 1) * 128] = piece
            top = jnp.maximum(top, piece)
        mx[...] = top

    def mix(slot, j):
        start = pl.multiple_of(j * CHUNK, CHUNK)
        top = tb[...]
        weights = [
            jnp.exp2(sc[slot, j, :, part * 128 : (part + 1) * 128] * SCALE - top).astype(
                jnp.bfloat16
            )
            for part in range(CHUNK // 128)
        ]
        acc[...] += jnp.dot(
            jnp.concatenate(weights, axis=1),
            va[pl.ds(start, CHUNK), :],
            preferred_element_type=jnp.float32,
        )

    def start_mix():
        top = jnp.max(mx[...], axis=1, keepdims=True) * SCALE
        tb[...] = jnp.broadcast_to(top, (ROWS, 128))
        acc[...] = jnp.zeros((ROWS, 256), jnp.float32)

    def close_tile(tile):
        total = acc[:, 128:256]
        result = acc[:, 0:128] / total
        spread = tb[...] + jnp.log2(total)
        stats = jnp.zeros((PART, 128), jnp.float32)
        for head in range(GROUP_HEADS):
            rows = slice(head * PART, (head + 1) * PART)
            out_ref[tile, :, head * 128 : (head + 1) * 128] = result[rows].astype(jnp.bfloat16)
            level = spread[rows]
            high = level.astype(jnp.bfloat16).astype(jnp.float32)
            rest = level - high
            middle = rest.astype(jnp.bfloat16).astype(jnp.float32)
            low = rest - middle
            stats = jnp.where(lane == head, high, stats)
            stats = jnp.where(lane == 8 + head, middle, stats)
            stats = jnp.where(lane == 16 + head, low, stats)
        out_ref[tile, :, WIDTH : WIDTH + 128] = stats.astype(jnp.bfloat16)

    first = meta[88]
    open_tile(first)

    def first_step(j, carry):
        score(0, j)
        return carry

    lax.fori_loop(0, meta[104 + first], first_step, 0)
    start_mix()

    def one_tile(k, carry):
        tile = meta[88 + k]
        following = meta[88 + jnp.minimum(k + 1, TILES - 1)]
        open_tile(following)
        slot = lax.rem(k, 2)

        def step(j, inner_carry):
            score(1 - slot, j)
            mix(slot, j)
            return inner_carry

        lax.fori_loop(0, meta[104 + tile], step, 0)
        close_tile(tile)
        start_mix()
        return carry

    lax.fori_loop(0, TILES, one_tile, 0)


def attend(meta, q, own, other):
    return pl.pallas_call(
        attend_kernel,
        out_shape=jax.ShapeDtypeStruct((TILES, PART, WIDTH + 128), jnp.bfloat16),
        grid_spec=pltpu.PrefetchScalarGridSpec(
            num_scalar_prefetch=1,
            grid=(),
            in_specs=[pl.BlockSpec(memory_space=pltpu.VMEM)] * 3,
            out_specs=pl.BlockSpec(memory_space=pltpu.VMEM),
            scratch_shapes=[
                pltpu.VMEM((ROWS, 128), jnp.bfloat16),
                pltpu.VMEM((KEYS, 128), jnp.bfloat16),
                pltpu.VMEM((KEYS, 256), jnp.bfloat16),
                pltpu.VMEM((8, KEYS), jnp.int32),
                pltpu.VMEM((ROWS, 128), jnp.int32),
                pltpu.VMEM((2, KEYS // CHUNK, ROWS, CHUNK), jnp.float32),
                pltpu.VMEM((ROWS, 128), jnp.float32),
                pltpu.VMEM((ROWS, 128), jnp.float32),
                pltpu.VMEM((ROWS, 256), jnp.float32),
            ],
        ),
        compiler_params=pltpu.CompilerParams(vmem_limit_bytes=48 * 1024 * 1024),
        name="attend",
    )(meta, q, own, other)


def merge_kernel(parts, out_ref):
    stats = [parts[x, :, WIDTH : WIDTH + 128].astype(jnp.float32) for x in range(NX)]
    for head in range(GROUP_HEADS):
        levels = [
            (s[:, head : head + 1] + s[:, 8 + head : 9 + head]) + s[:, 16 + head : 17 + head]
            for s in stats
        ]
        top = levels[0]
        for level in levels[1:]:
            top = jnp.maximum(top, level)
        shares = [jnp.exp2(level - top) for level in levels]
        total = shares[0]
        for share in shares[1:]:
            total = total + share
        columns = slice(head * 128, (head + 1) * 128)
        mixed = sum(
            parts[x, :, columns].astype(jnp.float32) * (share / total)
            for x, share in enumerate(shares)
        )
        for z in range(NZ):
            out_ref[z, :, columns] = mixed[z * PIECE : (z + 1) * PIECE].astype(jnp.bfloat16)


def merge(parts):
    return pl.pallas_call(
        merge_kernel,
        out_shape=jax.ShapeDtypeStruct((NZ, PIECE, WIDTH), jnp.bfloat16),
        name="merge",
    )(parts)


def schedule(block_order):
    table = block_order.reshape(NZL, NX, NY, 2)
    key_block = lax.dynamic_index_in_dim(table, lax.axis_index("x"), 1, keepdims=False)
    key_block = key_block.transpose(1, 0, 2).reshape(NB)
    query_block = lax.dynamic_index_in_dim(table, lax.axis_index("y"), 2, keepdims=False)
    query_block = query_block.transpose(1, 0, 2).reshape(TILES)
    rank = jnp.sum((key_block[None, :] < key_block[:, None]).astype(jnp.int32), axis=1)
    numbers = jnp.arange(NB, dtype=jnp.int32)
    in_order = jnp.sum(
        jnp.where(rank[None, :] == numbers[:, None], key_block[None, :], 0), axis=1
    )
    seen = jnp.sum((key_block[None, :] <= query_block[:, None]).astype(jnp.int32), axis=1)
    chunks = jnp.maximum((seen * BLOCK_TOKENS + CHUNK - 1) // CHUNK, 1)
    tiles = jnp.arange(TILES, dtype=jnp.int32)
    weight = chunks * TILES + tiles
    place = jnp.sum((weight[None, :] > weight[:, None]).astype(jnp.int32), axis=1)
    tile_at = jnp.sum(jnp.where(place[None, :] == tiles[:, None], tiles[None, :], 0), axis=1)
    head = jnp.broadcast_to(lax.axis_index("core"), (8,)).astype(jnp.int32)
    return jnp.concatenate([head, rank, in_order, query_block, tile_at, chunks])


def ring(shift, size):
    return [(i, (i + shift) % size) for i in range(size)]


def over(x, axes):
    return lax.all_to_all(x, axes, split_axis=0, concat_axis=0, tiled=True)


def on_device(queries, keys, values, block_order):
    z_axes = ("zl", "zh")
    kv = jnp.concatenate(
        [keys.reshape(PIECE, NZ, HEAD_DIMENSION), values.reshape(PIECE, NZ, HEAD_DIMENSION)],
        axis=2,
    ).transpose(1, 0, 2)
    kv = over(kv, z_axes).reshape(TOKENS, 256)
    q = over(queries.reshape(PIECE, NZ, WIDTH).transpose(1, 0, 2), z_axes)
    own = over(jnp.broadcast_to(kv[None], (NY, TOKENS, 256)), "y").reshape(NB, PART, 256)
    q = over(jnp.broadcast_to(q.reshape(1, TOKENS, WIDTH), (NX, TOKENS, WIDTH)), "x")
    other = lax.ppermute(own, "core", ring(1, 2))
    meta = schedule(block_order)
    parts = attend(meta, q.reshape(TILES, PART, WIDTH), own, other)
    parts = over(parts.reshape(NX, TOKENS, WIDTH + 128), "x")
    attended = over(merge(parts), z_axes)
    return attended.transpose(1, 0, 2).reshape(PIECE, NZ * WIDTH)


def solution(mesh):
    fine = Mesh(mesh.devices.reshape(NZL, NX, NY, NZH, 2), AXES)
    rows = P(AXES, None)
    return jax.shard_map(
        on_device, mesh=fine, in_specs=(rows, rows, rows, P()), out_specs=rows, check_vma=False
    )
```

```python
import jax
import jax.numpy as jnp
from jax import lax
from jax.experimental import pallas as pl
from jax.experimental.pallas import tpu as pltpu
from jax.sharding import Mesh, PartitionSpec as P


HEAD_DIMENSION = 128
GROUP_HEADS = 8
PIECE = 20
BLOCK_TOKENS = 80
NX, NY, NZL, NZH = 4, 8, 2, 4
NZ = NZL * NZH
AXES = ("zl", "x", "y", "zh", "core")
LOG2E = 1.4426950408889634
SCALE = HEAD_DIMENSION ** (-0.5) * LOG2E
HIDDEN = -1e30
NB = NZL * NY * 2
KEYS = NB * BLOCK_TOKENS
TOKENS = NZ * PIECE
WIDTH = GROUP_HEADS * HEAD_DIMENSION
PART = 2 * PIECE
TILES = NX * NZL * 2
ROWS = GROUP_HEADS * PART
CHUNK = 512
STRIP = 160


def attend_kernel(
    meta, q_ref, own_ref, other_ref, out_ref, qa, ka, va, kp, qp, sc_even, sc_odd, mx, tb, acc
):
    core = meta[0]

    def load_block(block, carry):
        rank = meta[8 + block]
        both = jnp.concatenate(
            [own_ref[block].astype(jnp.float32), other_ref[block].astype(jnp.float32)], axis=0
        ).astype(jnp.bfloat16)
        start = pl.multiple_of(rank * BLOCK_TOKENS, 16)
        ka[pl.ds(start, BLOCK_TOKENS), :] = both[:, 0:128]
        va[pl.ds(start, BLOCK_TOKENS), 0:128] = both[:, 128:256]
        return carry

    lax.fori_loop(0, NB, load_block, 0, unroll=4)
    va[:, 128:256] = jnp.ones((KEYS, 128), jnp.bfloat16)
    column = lax.broadcasted_iota(jnp.int32, (8, KEYS), 1)
    rank_of = column // BLOCK_TOKENS
    inner = column % BLOCK_TOKENS
    side = inner // PART
    inner = inner % PART
    key_core = jnp.where(side == 0, core, 1 - core)
    key_pos = (inner // PIECE) * PART + inner % PIECE + key_core * PIECE
    base = jnp.zeros((8, KEYS), jnp.int32)
    for rank in range(NB):
        base = jnp.where(rank_of == rank, meta[40 + rank], base)
    kp[...] = base * BLOCK_TOKENS + key_pos

    row = lax.broadcasted_iota(jnp.int32, (PART, 128), 0)
    row_offset = (row // PIECE) * PART + row % PIECE + core * PIECE
    lane = lax.broadcasted_iota(jnp.int32, (PART, 128), 1)
    hidden_row = jnp.full((ROWS, 128), -3e38, jnp.float32)

    def open_tile(tile):
        heads = [
            q_ref[tile, :, head * 128 : (head + 1) * 128].astype(jnp.float32)
            for head in range(GROUP_HEADS)
        ]
        qa[...] = jnp.concatenate(heads, axis=0).astype(jnp.bfloat16)
        pos = row_offset + meta[72 + tile] * BLOCK_TOKENS
        qp[...] = jnp.concatenate([pos] * GROUP_HEADS, axis=0)
        mx[...] = hidden_row

    def both(score_to, mix_from, j):
        start = pl.multiple_of(j * CHUNK, CHUNK)
        parts = [slice(part * 128, (part + 1) * 128) for part in range(CHUNK // 128)]
        keys = ka[pl.ds(start, CHUNK), :]
        key_pos = [
            kp[0:1, pl.ds(pl.multiple_of(start + part * 128, 128), 128)]
            for part in range(CHUNK // 128)
        ]
        values = va[pl.ds(start, CHUNK), :]
        for at in range(0, ROWS, STRIP):
            rows = slice(at, at + STRIP)
            if mix_from is not None:
                level = tb[rows, :]
                weights = [
                    jnp.exp2(mix_from[j, rows, part] * SCALE - level).astype(jnp.bfloat16)
                    for part in parts
                ]
            s = lax.dot_general(
                qa[rows, :], keys, (((1,), (1,)), ((), ())), preferred_element_type=jnp.float32
            )
            if mix_from is not None:
                acc[rows, :] += jnp.dot(
                    jnp.concatenate(weights, axis=1), values, preferred_element_type=jnp.float32
                )
            top = mx[rows, :]
            query_pos = qp[rows, :]
            for part, pos in zip(parts, key_pos):
                piece = jnp.where(pos <= query_pos, s[:, part], HIDDEN)
                score_to[j, rows, part] = piece
                top = jnp.maximum(top, piece)
            mx[rows, :] = top

    def start_mix():
        top = jnp.max(mx[...], axis=1, keepdims=True) * SCALE
        tb[...] = jnp.broadcast_to(top, (ROWS, 128))
        acc[...] = jnp.zeros((ROWS, 256), jnp.float32)

    def close_tile(tile):
        total = acc[:, 128:256]
        result = acc[:, 0:128] / total
        spread = tb[...] + jnp.log2(total)
        stats = jnp.zeros((PART, 128), jnp.float32)
        for head in range(GROUP_HEADS):
            rows = slice(head * PART, (head + 1) * PART)
            out_ref[tile, :, head * 128 : (head + 1) * 128] = result[rows].astype(jnp.bfloat16)
            level = spread[rows]
            high = level.astype(jnp.bfloat16).astype(jnp.float32)
            rest = level - high
            middle = rest.astype(jnp.bfloat16).astype(jnp.float32)
            low = rest - middle
            stats = jnp.where(lane == head, high, stats)
            stats = jnp.where(lane == 8 + head, middle, stats)
            stats = jnp.where(lane == 16 + head, low, stats)
        out_ref[tile, :, WIDTH : WIDTH + 128] = stats.astype(jnp.bfloat16)

    first = meta[88]
    open_tile(first)

    def first_step(j, carry):
        both(sc_even, None, j)
        return carry

    lax.fori_loop(0, meta[104 + first], first_step, 0)
    start_mix()

    def two_tiles(pair, carry):
        for odd in range(2):
            k = pair * 2 + odd
            tile = meta[88 + k]
            open_tile(meta[88 + jnp.minimum(k + 1, TILES - 1)])
            mix_from, score_to = (sc_odd, sc_even) if odd else (sc_even, sc_odd)

            def step(j, inner_carry):
                both(score_to, mix_from, j)
                return inner_carry

            lax.fori_loop(0, meta[104 + tile], step, 0)
            close_tile(tile)
            start_mix()
        return carry

    lax.fori_loop(0, TILES // 2, two_tiles, 0)


def attend(meta, q, own, other):
    return pl.pallas_call(
        attend_kernel,
        out_shape=jax.ShapeDtypeStruct((TILES, PART, WIDTH + 128), jnp.bfloat16),
        grid_spec=pltpu.PrefetchScalarGridSpec(
            num_scalar_prefetch=1,
            grid=(),
            in_specs=[pl.BlockSpec(memory_space=pltpu.VMEM)] * 3,
            out_specs=pl.BlockSpec(memory_space=pltpu.VMEM),
            scratch_shapes=[
                pltpu.VMEM((ROWS, 128), jnp.bfloat16),
                pltpu.VMEM((KEYS, 128), jnp.bfloat16),
                pltpu.VMEM((KEYS, 256), jnp.bfloat16),
                pltpu.VMEM((8, KEYS), jnp.int32),
                pltpu.VMEM((ROWS, 128), jnp.int32),
                pltpu.VMEM((KEYS // CHUNK, ROWS, CHUNK), jnp.float32),
                pltpu.VMEM((KEYS // CHUNK, ROWS, CHUNK), jnp.float32),
                pltpu.VMEM((ROWS, 128), jnp.float32),
                pltpu.VMEM((ROWS, 128), jnp.float32),
                pltpu.VMEM((ROWS, 256), jnp.float32),
            ],
        ),
        compiler_params=pltpu.CompilerParams(vmem_limit_bytes=48 * 1024 * 1024),
        name="attend",
    )(meta, q, own, other)


def merge_kernel(parts, out_ref):
    stats = [parts[x, :, WIDTH : WIDTH + 128].astype(jnp.float32) for x in range(NX)]
    for head in range(GROUP_HEADS):
        levels = [
            (s[:, head : head + 1] + s[:, 8 + head : 9 + head]) + s[:, 16 + head : 17 + head]
            for s in stats
        ]
        top = levels[0]
        for level in levels[1:]:
            top = jnp.maximum(top, level)
        shares = [jnp.exp2(level - top) for level in levels]
        total = shares[0]
        for share in shares[1:]:
            total = total + share
        columns = slice(head * 128, (head + 1) * 128)
        mixed = sum(
            parts[x, :, columns].astype(jnp.float32) * (share / total)
            for x, share in enumerate(shares)
        )
        for z in range(NZ):
            out_ref[z, :, columns] = mixed[z * PIECE : (z + 1) * PIECE].astype(jnp.bfloat16)


def merge(parts):
    return pl.pallas_call(
        merge_kernel,
        out_shape=jax.ShapeDtypeStruct((NZ, PIECE, WIDTH), jnp.bfloat16),
        name="merge",
    )(parts)


def schedule(block_order):
    table = block_order.reshape(NZL, NX, NY, 2)
    key_block = lax.dynamic_index_in_dim(table, lax.axis_index("x"), 1, keepdims=False)
    key_block = key_block.transpose(1, 0, 2).reshape(NB)
    query_block = lax.dynamic_index_in_dim(table, lax.axis_index("y"), 2, keepdims=False)
    query_block = query_block.transpose(1, 0, 2).reshape(TILES)
    rank = jnp.sum((key_block[None, :] < key_block[:, None]).astype(jnp.int32), axis=1)
    numbers = jnp.arange(NB, dtype=jnp.int32)
    in_order = jnp.sum(
        jnp.where(rank[None, :] == numbers[:, None], key_block[None, :], 0), axis=1
    )
    seen = jnp.sum((key_block[None, :] <= query_block[:, None]).astype(jnp.int32), axis=1)
    chunks = jnp.maximum((seen * BLOCK_TOKENS + CHUNK - 1) // CHUNK, 1)
    tiles = jnp.arange(TILES, dtype=jnp.int32)
    weight = chunks * TILES + tiles
    place = jnp.sum((weight[None, :] > weight[:, None]).astype(jnp.int32), axis=1)
    tile_at = jnp.sum(jnp.where(place[None, :] == tiles[:, None], tiles[None, :], 0), axis=1)
    head = jnp.broadcast_to(lax.axis_index("core"), (8,)).astype(jnp.int32)
    return jnp.concatenate([head, rank, in_order, query_block, tile_at, chunks])


def ring(shift, size):
    return [(i, (i + shift) % size) for i in range(size)]


def over(x, axes):
    return lax.all_to_all(x, axes, split_axis=0, concat_axis=0, tiled=True)


def on_device(queries, keys, values, block_order):
    z_axes = ("zl", "zh")
    packed = jnp.concatenate(
        [
            queries.reshape(PIECE, NZ, WIDTH),
            keys.reshape(PIECE, NZ, HEAD_DIMENSION),
            values.reshape(PIECE, NZ, HEAD_DIMENSION),
        ],
        axis=2,
    ).transpose(1, 0, 2)
    packed = over(packed, z_axes).reshape(TOKENS, WIDTH + 256)
    kv = packed[:, WIDTH:]
    q = over(jnp.broadcast_to(packed[None, :, :WIDTH], (NX, TOKENS, WIDTH)), "x")
    own = lax.all_gather(kv, "y", axis=0, tiled=True)
    own = own.reshape(NB, PART, 256)
    other = lax.ppermute(own, "core", ring(1, 2))
    meta = schedule(block_order)
    parts = attend(meta, q.reshape(TILES, PART, WIDTH), own, other)
    parts = over(parts.reshape(NX, TOKENS, WIDTH + 128), "x")
    attended = over(merge(parts), z_axes)
    return attended.transpose(1, 0, 2).reshape(PIECE, NZ * WIDTH)


def solution(mesh):
    fine = Mesh(mesh.devices.reshape(NZL, NX, NY, NZH, 2), AXES)
    rows = P(AXES, None)
    return jax.shard_map(
        on_device, mesh=fine, in_specs=(rows, rows, rows, P()), out_specs=rows, check_vma=False
    )
```

```python
import jax
import jax.numpy as jnp
from jax import lax
from jax.experimental import pallas as pl
from jax.experimental.pallas import tpu as pltpu
from jax.sharding import Mesh, PartitionSpec as P


HEAD_DIMENSION = 128
GROUP_HEADS = 8
PIECE = 20
BLOCK_TOKENS = 80
NX, NY, NZL, NZH = 4, 8, 2, 4
NZ = NZL * NZH
AXES = ("zl", "x", "y", "zh", "core")
LOG2E = 1.4426950408889634
SCALE = HEAD_DIMENSION ** (-0.5) * LOG2E
HIDDEN = -1e30
NB = NZL * NY * 2
KEYS = NB * BLOCK_TOKENS
TOKENS = NZ * PIECE
WIDTH = GROUP_HEADS * HEAD_DIMENSION
PART = 2 * PIECE
OWN_TILES = NZL * 2
TILES = NX * OWN_TILES
ROWS = GROUP_HEADS * PART
CHUNK = 512
STRIP = 160


def attend_kernel(
    tiles, first_place, meta, q_ref, own_ref, other_ref, kp, out_ref, qa, ka, va, qp, sc_even,
    sc_odd, mx, tb, acc
):
    core = meta[0]

    def load_block(block, carry):
        rank = meta[8 + block]
        both = jnp.concatenate(
            [own_ref[block].astype(jnp.float32), other_ref[block].astype(jnp.float32)], axis=0
        ).astype(jnp.bfloat16)
        start = pl.multiple_of(rank * BLOCK_TOKENS, 16)
        ka[pl.ds(start, BLOCK_TOKENS), :] = both[:, 0:128]
        va[pl.ds(start, BLOCK_TOKENS), 0:128] = both[:, 128:256]
        return carry

    lax.fori_loop(0, NB, load_block, 0, unroll=4)
    va[:, 128:256] = jnp.ones((KEYS, 128), jnp.bfloat16)
    row = lax.broadcasted_iota(jnp.int32, (PART, 128), 0)
    row_offset = (row // PIECE) * PART + row % PIECE + core * PIECE
    lane = lax.broadcasted_iota(jnp.int32, (PART, 128), 1)
    hidden_row = jnp.full((ROWS, 128), -3e38, jnp.float32)

    def open_tile(tile):
        heads = [
            q_ref[tile, :, head * 128 : (head + 1) * 128].astype(jnp.float32)
            for head in range(GROUP_HEADS)
        ]
        qa[...] = jnp.concatenate(heads, axis=0).astype(jnp.bfloat16)
        pos = row_offset + meta[72 + tile] * BLOCK_TOKENS
        qp[...] = jnp.concatenate([pos] * GROUP_HEADS, axis=0)
        mx[...] = hidden_row

    def both(score_to, mix_from, j):
        start = pl.multiple_of(j * CHUNK, CHUNK)
        parts = [slice(part * 128, (part + 1) * 128) for part in range(CHUNK // 128)]
        keys = ka[pl.ds(start, CHUNK), :]
        key_pos = [
            kp[0:1, pl.ds(pl.multiple_of(start + part * 128, 128), 128)]
            for part in range(CHUNK // 128)
        ]
        values = va[pl.ds(start, CHUNK), :]
        for at in range(0, ROWS, STRIP):
            rows = slice(at, at + STRIP)
            if mix_from is not None:
                level = tb[rows, :]
                weights = [
                    jnp.exp2(mix_from[j, rows, part] * SCALE - level).astype(jnp.bfloat16)
                    for part in parts
                ]
            s = lax.dot_general(
                qa[rows, :], keys, (((1,), (1,)), ((), ())), preferred_element_type=jnp.float32
            )
            if mix_from is not None:
                acc[rows, :] += jnp.dot(
                    jnp.concatenate(weights, axis=1), values, preferred_element_type=jnp.float32
                )
            top = mx[rows, :]
            query_pos = qp[rows, :]
            for part, pos in zip(parts, key_pos):
                piece = jnp.where(pos <= query_pos, s[:, part], HIDDEN)
                score_to[j, rows, part] = piece
                top = jnp.maximum(top, piece)
            mx[rows, :] = top

    def start_mix():
        top = jnp.max(mx[...], axis=1, keepdims=True) * SCALE
        tb[...] = jnp.broadcast_to(top, (ROWS, 128))
        acc[...] = jnp.zeros((ROWS, 256), jnp.float32)

    def close_tile(tile):
        place = lax.rem(tile, OWN_TILES) if tiles == OWN_TILES else tile
        total = acc[:, 128:256]
        result = acc[:, 0:128] / total
        spread = tb[...] + jnp.log2(total)
        stats = jnp.zeros((PART, 128), jnp.float32)
        for head in range(GROUP_HEADS):
            rows = slice(head * PART, (head + 1) * PART)
            out_ref[place, :, head * 128 : (head + 1) * 128] = result[rows].astype(jnp.bfloat16)
            level = spread[rows]
            high = level.astype(jnp.bfloat16).astype(jnp.float32)
            rest = level - high
            middle = rest.astype(jnp.bfloat16).astype(jnp.float32)
            low = rest - middle
            stats = jnp.where(lane == head, high, stats)
            stats = jnp.where(lane == 8 + head, middle, stats)
            stats = jnp.where(lane == 16 + head, low, stats)
        out_ref[place, :, WIDTH : WIDTH + 128] = stats.astype(jnp.bfloat16)

    first = meta[88 + first_place]
    open_tile(first)

    def first_step(j, carry):
        both(sc_even, None, j)
        return carry

    lax.fori_loop(0, meta[104 + first], first_step, 0)
    start_mix()

    if tiles == TILES - OWN_TILES:
        own_x = meta[1]
        out_ref[pl.ds(own_x * OWN_TILES, OWN_TILES)] = jnp.zeros(
            (OWN_TILES, PART, WIDTH + 128), jnp.bfloat16
        )

    def two_tiles(pair, carry):
        for odd in range(2):
            k = pair * 2 + odd
            tile = meta[88 + first_place + k]
            open_tile(meta[88 + first_place + jnp.minimum(k + 1, tiles - 1)])
            mix_from, score_to = (sc_odd, sc_even) if odd else (sc_even, sc_odd)

            def step(j, inner_carry):
                both(score_to, mix_from, j)
                return inner_carry

            lax.fori_loop(0, meta[104 + tile], step, 0)
            close_tile(tile)
            start_mix()
        return carry

    lax.fori_loop(0, tiles // 2, two_tiles, 0)


def attend(mine, meta, q, own, other, key_pos):
    tiles = OWN_TILES if mine else TILES - OWN_TILES
    first_place = TILES - OWN_TILES if mine else 0

    def kernel(*refs):
        attend_kernel(tiles, first_place, *refs)

    return pl.pallas_call(
        kernel,
        out_shape=jax.ShapeDtypeStruct(
            (OWN_TILES if mine else TILES, PART, WIDTH + 128), jnp.bfloat16
        ),
        grid_spec=pltpu.PrefetchScalarGridSpec(
            num_scalar_prefetch=1,
            grid=(),
            in_specs=[pl.BlockSpec(memory_space=pltpu.VMEM)] * 4,
            out_specs=pl.BlockSpec(memory_space=pltpu.VMEM),
            scratch_shapes=[
                pltpu.VMEM((ROWS, 128), jnp.bfloat16),
                pltpu.VMEM((KEYS, 128), jnp.bfloat16),
                pltpu.VMEM((KEYS, 256), jnp.bfloat16),
                pltpu.VMEM((ROWS, 128), jnp.int32),
                pltpu.VMEM((KEYS // CHUNK, ROWS, CHUNK), jnp.float32),
                pltpu.VMEM((KEYS // CHUNK, ROWS, CHUNK), jnp.float32),
                pltpu.VMEM((ROWS, 128), jnp.float32),
                pltpu.VMEM((ROWS, 128), jnp.float32),
                pltpu.VMEM((ROWS, 256), jnp.float32),
            ],
        ),
        compiler_params=pltpu.CompilerParams(vmem_limit_bytes=48 * 1024 * 1024),
        name="attend_own" if mine else "attend_rest",
    )(meta, q, own, other, key_pos)


def merge_kernel(own_x, parts, mine, out_ref):
    levels = []
    for x in range(NX):
        stats = jnp.where(
            own_x[0] == x,
            mine[:, WIDTH : WIDTH + 128].astype(jnp.float32),
            parts[x, :, WIDTH : WIDTH + 128].astype(jnp.float32),
        )
        levels.append((stats + pltpu.roll(stats, 120, 1)) + pltpu.roll(stats, 112, 1))
    top = levels[0]
    for level in levels[1:]:
        top = jnp.maximum(top, level)
    shares = [jnp.exp2(level - top) for level in levels]
    total = shares[0]
    for share in shares[1:]:
        total = total + share
    shares = [share / total for share in shares]
    keep = [jnp.where(own_x[0] == x, 0.0, share) for x, share in enumerate(shares)]
    home = sum(share - other for share, other in zip(shares, keep))
    for head in range(GROUP_HEADS):
        columns = slice(head * 128, (head + 1) * 128)
        mixed = mine[:, columns].astype(jnp.float32) * home[:, head : head + 1]
        for x in range(NX):
            mixed += parts[x, :, columns].astype(jnp.float32) * keep[x][:, head : head + 1]
        for z in range(NZ):
            out_ref[z, :, columns] = mixed[z * PIECE : (z + 1) * PIECE].astype(jnp.bfloat16)


def merge(own_x, parts, mine):
    return pl.pallas_call(
        merge_kernel,
        out_shape=jax.ShapeDtypeStruct((NZ, PIECE, WIDTH), jnp.bfloat16),
        in_specs=[
            pl.BlockSpec(memory_space=pltpu.SMEM),
            pl.BlockSpec(memory_space=pltpu.VMEM),
            pl.BlockSpec(memory_space=pltpu.VMEM),
        ],
        name="merge",
    )(own_x, parts, mine)


def schedule(block_order):
    table = block_order.reshape(NZL, NX, NY, 2)
    key_block = lax.dynamic_index_in_dim(table, lax.axis_index("x"), 1, keepdims=False)
    key_block = key_block.transpose(1, 0, 2).reshape(NB)
    query_block = lax.dynamic_index_in_dim(table, lax.axis_index("y"), 2, keepdims=False)
    query_block = query_block.transpose(1, 0, 2).reshape(TILES)
    rank = jnp.sum((key_block[None, :] < key_block[:, None]).astype(jnp.int32), axis=1)
    numbers = jnp.arange(NB, dtype=jnp.int32)
    in_order = jnp.sum(
        jnp.where(rank[None, :] == numbers[:, None], key_block[None, :], 0), axis=1
    )
    seen = jnp.sum((key_block[None, :] <= query_block[:, None]).astype(jnp.int32), axis=1)
    chunks = jnp.maximum((seen * BLOCK_TOKENS + CHUNK - 1) // CHUNK, 1)
    tiles = jnp.arange(TILES, dtype=jnp.int32)
    own_x = lax.axis_index("x")
    remote = (tiles // OWN_TILES != own_x).astype(jnp.int32)
    weight = (remote * 64 + chunks) * TILES + tiles
    place = jnp.sum((weight[None, :] > weight[:, None]).astype(jnp.int32), axis=1)
    tile_at = jnp.sum(jnp.where(place[None, :] == tiles[:, None], tiles[None, :], 0), axis=1)
    spot = jnp.arange(BLOCK_TOKENS, dtype=jnp.int32)
    core = lax.axis_index("core")
    key_core = jnp.where(spot < PART, core, 1 - core)
    inner = spot % PART
    place = (inner // PIECE) * PART + inner % PIECE + key_core * PIECE
    key_pos = in_order[:, None] * BLOCK_TOKENS + place[None, :]
    head = jnp.concatenate([core.reshape(1), own_x.reshape(1), jnp.zeros((6,), jnp.int32)])
    meta = jnp.concatenate([head, rank, in_order, query_block, tile_at, chunks])
    return meta, key_pos.reshape(1, KEYS)


def ring(shift, size):
    return [(i, (i + shift) % size) for i in range(size)]


def over(x, axes):
    return lax.all_to_all(x, axes, split_axis=0, concat_axis=0, tiled=True)


def on_device(queries, keys, values, block_order):
    z_axes = ("zl", "zh")
    packed = jnp.concatenate(
        [
            queries.reshape(PIECE, NZ, WIDTH),
            keys.reshape(PIECE, NZ, HEAD_DIMENSION),
            values.reshape(PIECE, NZ, HEAD_DIMENSION),
        ],
        axis=2,
    ).transpose(1, 0, 2)
    packed = over(packed, z_axes).reshape(TOKENS, WIDTH + 256)
    kv = packed[:, WIDTH:]
    q = over(jnp.broadcast_to(packed[None, :, :WIDTH], (NX, TOKENS, WIDTH)), "x")
    own = lax.all_gather(kv, "y", axis=0, tiled=True)
    own = own.reshape(NB, PART, 256)
    other = lax.ppermute(own, "core", ring(1, 2))
    meta, key_pos = schedule(block_order)
    q = q.reshape(TILES, PART, WIDTH)
    parts = attend(False, meta, q, own, other, key_pos)
    parts = over(parts.reshape(NX, TOKENS, WIDTH + 128), "x")
    mine = attend(True, meta, q, own, other, key_pos).reshape(TOKENS, WIDTH + 128)
    attended = over(merge(meta[1:2], parts, mine), z_axes)
    return attended.transpose(1, 0, 2).reshape(PIECE, NZ * WIDTH)


def solution(mesh):
    fine = Mesh(mesh.devices.reshape(NZL, NX, NY, NZH, 2), AXES)
    rows = P(AXES, None)
    return jax.shard_map(
        on_device, mesh=fine, in_specs=(rows, rows, rows, P()), out_specs=rows, check_vma=False
    )
```

```python
import functools

import jax
import jax.numpy as jnp
from jax import lax
from jax.experimental import pallas as pl
from jax.experimental.pallas import tpu as pltpu
from jax.sharding import Mesh, PartitionSpec as P


HEAD_DIMENSION = 128
GROUP_HEADS = 8
PIECE = 20
BLOCK_TOKENS = 80
NX, NY, NZL, NZH = 4, 8, 2, 4
NZ = NZL * NZH
AXES = ("zl", "x", "y", "zh", "core")
LOG2E = 1.4426950408889634
SCALE = HEAD_DIMENSION ** (-0.5) * LOG2E
HIDDEN = -1e30
NB = NZL * NY * 2
KEYS = NB * BLOCK_TOKENS
TOKENS = NZ * PIECE
WIDTH = GROUP_HEADS * HEAD_DIMENSION
PART = 2 * PIECE
OWN_TILES = NZL * 2
TILES = NX * OWN_TILES
ROWS = GROUP_HEADS * PART
CHUNK = 512
STRIP = 160


def attend_kernel(
    tiles, first_place, meta, q_ref, own_ref, other_ref, kp, *refs
):
    out_refs = refs[: tiles // OWN_TILES]
    out_ref, qa, ka, va, qp, sc_even, sc_odd, mx, tb, acc = refs[tiles // OWN_TILES :]
    core = meta[0]
    own_x = meta[1]

    def load_block(block, carry):
        rank = meta[8 + block]
        both = jnp.concatenate(
            [own_ref[block].astype(jnp.float32), other_ref[block].astype(jnp.float32)], axis=0
        ).astype(jnp.bfloat16)
        start = pl.multiple_of(rank * BLOCK_TOKENS, 16)
        ka[pl.ds(start, BLOCK_TOKENS), :] = both[:, 0:128]
        va[pl.ds(start, BLOCK_TOKENS), 0:128] = both[:, 128:256]
        return carry

    lax.fori_loop(0, NB, load_block, 0, unroll=4)
    va[:, 128:256] = jnp.ones((KEYS, 128), jnp.bfloat16)
    row = lax.broadcasted_iota(jnp.int32, (PART, 128), 0)
    row_offset = (row // PIECE) * PART + row % PIECE + core * PIECE
    lane = lax.broadcasted_iota(jnp.int32, (PART, 128), 1)
    hidden_row = jnp.full((ROWS, 128), -3e38, jnp.float32)

    def open_tile(tile):
        heads = [
            q_ref[tile, :, head * 128 : (head + 1) * 128].astype(jnp.float32)
            for head in range(GROUP_HEADS)
        ]
        qa[...] = jnp.concatenate(heads, axis=0).astype(jnp.bfloat16)
        pos = row_offset + meta[72 + tile] * BLOCK_TOKENS
        qp[...] = jnp.concatenate([pos] * GROUP_HEADS, axis=0)
        mx[...] = hidden_row

    def both(score_to, mix_from, masked, j):
        start = pl.multiple_of(j * CHUNK, CHUNK)
        parts = [slice(part * 128, (part + 1) * 128) for part in range(CHUNK // 128)]
        keys = ka[pl.ds(start, CHUNK), :]
        key_pos = [
            kp[0:1, pl.ds(pl.multiple_of(start + part * 128, 128), 128)]
            for part in range(CHUNK // 128)
        ]
        values = va[pl.ds(start, CHUNK), :]
        for at in range(0, ROWS, STRIP):
            rows = slice(at, at + STRIP)
            if mix_from is not None:
                level = tb[rows, :]
                weights = [
                    jnp.exp2(mix_from[j, rows, part] * SCALE - level).astype(jnp.bfloat16)
                    for part in parts
                ]
            s = lax.dot_general(
                qa[rows, :], keys, (((1,), (1,)), ((), ())), preferred_element_type=jnp.float32
            )
            if mix_from is not None:
                acc[rows, :] += jnp.dot(
                    jnp.concatenate(weights, axis=1), values, preferred_element_type=jnp.float32
                )
            top = mx[rows, :]
            query_pos = qp[rows, :]
            for part, pos in zip(parts, key_pos):
                piece = s[:, part]
                if masked:
                    piece = jnp.where(pos <= query_pos, piece, HIDDEN)
                score_to[j, rows, part] = piece
                top = jnp.maximum(top, piece)
            mx[rows, :] = top

    def start_mix():
        top = jnp.max(mx[...], axis=1, keepdims=True) * SCALE
        tb[...] = jnp.broadcast_to(top, (ROWS, 128))
        acc[...] = jnp.zeros((ROWS, 256), jnp.float32)

    def close_tile(tile):
        shift = lax.rem(own_x + NX - tile // OWN_TILES, NX)
        place = jnp.maximum(shift - 1, 0) * OWN_TILES + lax.rem(tile, OWN_TILES)
        total = acc[:, 128:256]
        result = acc[:, 0:128] / total
        spread = tb[...] + jnp.log2(total)
        stats = jnp.zeros((PART, 128), jnp.float32)
        for head in range(GROUP_HEADS):
            rows = slice(head * PART, (head + 1) * PART)
            out_ref[place, :, head * 128 : (head + 1) * 128] = result[rows].astype(jnp.bfloat16)
            level = spread[rows]
            high = level.astype(jnp.bfloat16).astype(jnp.float32)
            rest = level - high
            middle = rest.astype(jnp.bfloat16).astype(jnp.float32)
            low = rest - middle
            stats = jnp.where(lane == head, high, stats)
            stats = jnp.where(lane == 8 + head, middle, stats)
            stats = jnp.where(lane == 16 + head, low, stats)
        out_ref[place, :, WIDTH : WIDTH + 128] = stats.astype(jnp.bfloat16)

    first = meta[88 + first_place]
    open_tile(first)

    def run(score_to, mix_from, clear, count):
        def step(masked, j, carry):
            both(score_to, mix_from, masked, j)
            return carry

        lax.fori_loop(0, clear, functools.partial(step, False), 0)
        lax.fori_loop(clear, count, functools.partial(step, True), 0)

    run(sc_even, None, meta[120 + first], meta[104 + first])
    start_mix()

    def two_tiles(pair, carry):
        for odd in range(2):
            k = pair * 2 + odd
            tile = meta[88 + first_place + k]
            following = meta[88 + first_place + jnp.minimum(k + 1, tiles - 1)]
            open_tile(following)
            mix_from, score_to = (sc_odd, sc_even) if odd else (sc_even, sc_odd)
            run(score_to, mix_from, meta[120 + following], meta[104 + tile])
            close_tile(tile)
            start_mix()
        return carry

    lax.fori_loop(0, tiles // 2, two_tiles, 0)
    for number, target in enumerate(out_refs):
        target[...] = out_ref[number * OWN_TILES : (number + 1) * OWN_TILES]


def attend(mine, meta, q, own, other, key_pos):
    tiles = OWN_TILES if mine else TILES - OWN_TILES
    first_place = TILES - OWN_TILES if mine else 0

    def kernel(*refs):
        attend_kernel(tiles, first_place, *refs)

    return pl.pallas_call(
        kernel,
        out_shape=[jax.ShapeDtypeStruct((OWN_TILES, PART, WIDTH + 128), jnp.bfloat16)]
        * (tiles // OWN_TILES),
        grid_spec=pltpu.PrefetchScalarGridSpec(
            num_scalar_prefetch=1,
            grid=(),
            in_specs=[pl.BlockSpec(memory_space=pltpu.VMEM)] * 4,
            out_specs=[pl.BlockSpec(memory_space=pltpu.VMEM)] * (tiles // OWN_TILES),
            scratch_shapes=[
                pltpu.VMEM((tiles, PART, WIDTH + 128), jnp.bfloat16),
                pltpu.VMEM((ROWS, 128), jnp.bfloat16),
                pltpu.VMEM((KEYS, 128), jnp.bfloat16),
                pltpu.VMEM((KEYS, 256), jnp.bfloat16),
                pltpu.VMEM((ROWS, 128), jnp.int32),
                pltpu.VMEM((KEYS // CHUNK, ROWS, CHUNK), jnp.float32),
                pltpu.VMEM((KEYS // CHUNK, ROWS, CHUNK), jnp.float32),
                pltpu.VMEM((ROWS, 128), jnp.float32),
                pltpu.VMEM((ROWS, 128), jnp.float32),
                pltpu.VMEM((ROWS, 256), jnp.float32),
            ],
        ),
        compiler_params=pltpu.CompilerParams(vmem_limit_bytes=48 * 1024 * 1024),
        name="attend_own" if mine else "attend_rest",
    )(meta, q, own, other, key_pos)


def merge_kernel(*refs):
    parts, out_ref = refs[:NX], refs[NX]
    levels = []
    for part in parts:
        stats = part[:, WIDTH : WIDTH + 128].astype(jnp.float32)
        levels.append((stats + pltpu.roll(stats, 120, 1)) + pltpu.roll(stats, 112, 1))
    top = levels[0]
    for level in levels[1:]:
        top = jnp.maximum(top, level)
    shares = [jnp.exp2(level - top) for level in levels]
    total = shares[0]
    for share in shares[1:]:
        total = total + share
    shares = [share / total for share in shares]
    for head in range(GROUP_HEADS):
        columns = slice(head * 128, (head + 1) * 128)
        mixed = sum(
            part[:, columns].astype(jnp.float32) * share[:, head : head + 1]
            for part, share in zip(parts, shares)
        )
        for z in range(NZ):
            out_ref[z, :, columns] = mixed[z * PIECE : (z + 1) * PIECE].astype(jnp.bfloat16)


def merge(parts):
    return pl.pallas_call(
        merge_kernel,
        out_shape=jax.ShapeDtypeStruct((NZ, PIECE, WIDTH), jnp.bfloat16),
        name="merge",
    )(*parts)


def pack_kernel(q_ref, k_ref, v_ref, out_ref):
    for z in range(NZ):
        out_ref[z, :, 0:WIDTH] = q_ref[:, z * WIDTH : (z + 1) * WIDTH]
        columns = slice(z * HEAD_DIMENSION, (z + 1) * HEAD_DIMENSION)
        out_ref[z, :, WIDTH : WIDTH + 128] = k_ref[:, columns]
        out_ref[z, :, WIDTH + 128 : WIDTH + 256] = v_ref[:, columns]


def pack(queries, keys, values):
    return pl.pallas_call(
        pack_kernel,
        out_shape=jax.ShapeDtypeStruct((NZ, PIECE, WIDTH + 256), jnp.bfloat16),
        name="pack",
    )(queries, keys, values)


def schedule(block_order):
    table = block_order.reshape(NZL, NX, NY, 2)
    key_block = lax.dynamic_index_in_dim(table, lax.axis_index("x"), 1, keepdims=False)
    key_block = key_block.transpose(1, 0, 2).reshape(NB)
    query_block = lax.dynamic_index_in_dim(table, lax.axis_index("y"), 2, keepdims=False)
    query_block = query_block.transpose(1, 0, 2).reshape(TILES)
    rank = jnp.sum((key_block[None, :] < key_block[:, None]).astype(jnp.int32), axis=1)
    numbers = jnp.arange(NB, dtype=jnp.int32)
    in_order = jnp.sum(
        jnp.where(rank[None, :] == numbers[:, None], key_block[None, :], 0), axis=1
    )
    seen = jnp.sum((key_block[None, :] <= query_block[:, None]).astype(jnp.int32), axis=1)
    chunks = jnp.maximum((seen * BLOCK_TOKENS + CHUNK - 1) // CHUNK, 1)
    strict = jnp.sum((key_block[None, :] < query_block[:, None]).astype(jnp.int32), axis=1)
    clear = strict * BLOCK_TOKENS // CHUNK
    tiles = jnp.arange(TILES, dtype=jnp.int32)
    own_x = lax.axis_index("x")
    remote = (tiles // OWN_TILES != own_x).astype(jnp.int32)
    weight = (remote * 64 + chunks) * TILES + tiles
    place = jnp.sum((weight[None, :] > weight[:, None]).astype(jnp.int32), axis=1)
    tile_at = jnp.sum(jnp.where(place[None, :] == tiles[:, None], tiles[None, :], 0), axis=1)
    spot = jnp.arange(BLOCK_TOKENS, dtype=jnp.int32)
    core = lax.axis_index("core")
    key_core = jnp.where(spot < PART, core, 1 - core)
    inner = spot % PART
    place = (inner // PIECE) * PART + inner % PIECE + key_core * PIECE
    key_pos = in_order[:, None] * BLOCK_TOKENS + place[None, :]
    head = jnp.concatenate([core.reshape(1), own_x.reshape(1), jnp.zeros((6,), jnp.int32)])
    meta = jnp.concatenate([head, rank, in_order, query_block, tile_at, chunks, clear])
    return meta, key_pos.reshape(1, KEYS)


def ring(shift, size):
    return [(i, (i + shift) % size) for i in range(size)]


def over(x, axes):
    return lax.all_to_all(x, axes, split_axis=0, concat_axis=0, tiled=True)


def on_device(queries, keys, values, block_order):
    z_axes = ("zl", "zh")
    packed = pack(queries, keys, values)
    packed = over(packed, z_axes).reshape(TOKENS, WIDTH + 256)
    kv = packed[:, WIDTH:]
    q = over(jnp.broadcast_to(packed[None, :, :WIDTH], (NX, TOKENS, WIDTH)), "x")
    own = lax.all_gather(kv, "y", axis=0, tiled=True)
    own = own.reshape(NB, PART, 256)
    other = lax.ppermute(own, "core", ring(1, 2))
    meta, key_pos = schedule(block_order)
    q = q.reshape(TILES, PART, WIDTH)
    shape = (TOKENS, WIDTH + 128)
    rest = attend(False, meta, q, own, other, key_pos)
    parts = [
        lax.ppermute(rest[shift - 1].reshape(shape), "x", ring(-shift, NX)) for shift in (2, 1, 3)
    ]
    mine = attend(True, meta, q, own, other, key_pos)
    parts.append(mine[0].reshape(shape))
    attended = over(merge(parts), z_axes)
    return attended.transpose(1, 0, 2).reshape(PIECE, NZ * WIDTH)


def solution(mesh):
    fine = Mesh(mesh.devices.reshape(NZL, NX, NY, NZH, 2), AXES)
    rows = P(AXES, None)
    return jax.shard_map(
        on_device, mesh=fine, in_specs=(rows, rows, rows, P()), out_specs=rows, check_vma=False
    )
```

```python
import functools

import jax
import jax.numpy as jnp
from jax import lax
from jax.experimental import pallas as pl
from jax.experimental.pallas import tpu as pltpu
from jax.sharding import Mesh, PartitionSpec as P


HEAD_DIMENSION = 128
GROUP_HEADS = 8
PIECE = 20
BLOCK_TOKENS = 80
NX, NY, NZL, NZH = 4, 8, 2, 4
NZ = NZL * NZH
AXES = ("zl", "x", "y", "zh", "core")
LOG2E = 1.4426950408889634
SCALE = HEAD_DIMENSION ** (-0.5) * LOG2E
HIDDEN = -1e30
NB = NZL * NY * 2
KEYS = NB * BLOCK_TOKENS
TOKENS = NZ * PIECE
WIDTH = GROUP_HEADS * HEAD_DIMENSION
PART = 2 * PIECE
OWN_TILES = NZL * 2
TILES = NX * OWN_TILES
ROWS = GROUP_HEADS * PART
CHUNK = 512
STRIP = 160


def attend_kernel(
    tiles, first_place, meta, q_ref, own_ref, other_ref, kp, *refs
):
    out_refs = refs[: tiles // OWN_TILES]
    out_ref, qa, ka, va, qp, sc_even, sc_odd, mx, tb, acc = refs[tiles // OWN_TILES :]
    core = meta[0]
    own_x = meta[1]

    def load_block(block, carry):
        rank = meta[8 + block]
        both = jnp.concatenate(
            [own_ref[block].astype(jnp.float32), other_ref[block].astype(jnp.float32)], axis=0
        ).astype(jnp.bfloat16)
        start = pl.multiple_of(rank * BLOCK_TOKENS, 16)
        ka[pl.ds(start, BLOCK_TOKENS), :] = both[:, 0:128]
        va[pl.ds(start, BLOCK_TOKENS), 0:128] = both[:, 128:256]
        return carry

    lax.fori_loop(0, NB, load_block, 0, unroll=4)
    va[:, 128:256] = jnp.ones((KEYS, 128), jnp.bfloat16)
    row = lax.broadcasted_iota(jnp.int32, (PART, 128), 0)
    row_offset = (row // PIECE) * PART + row % PIECE + core * PIECE
    lane = lax.broadcasted_iota(jnp.int32, (PART, 128), 1)

    def open_tile(tile):
        heads = [
            q_ref[tile, :, head * 128 : (head + 1) * 128].astype(jnp.float32)
            for head in range(GROUP_HEADS)
        ]
        qa[...] = jnp.concatenate(heads, axis=0).astype(jnp.bfloat16)
        pos = row_offset + meta[72 + tile] * BLOCK_TOKENS
        qp[...] = jnp.concatenate([pos] * GROUP_HEADS, axis=0)

    def both(score_to, mix_from, count):
        width = count * CHUNK
        for at in range(0, ROWS, STRIP):
            rows = slice(at, at + STRIP)
            if mix_from is not None:
                level = tb[rows, :]
                weights = [
                    jnp.exp2(mix_from[rows, start : start + 128] * SCALE - level).astype(
                        jnp.bfloat16
                    )
                    for start in range(0, width, 128)
                ]
            s = lax.dot_general(
                qa[rows, :],
                ka[0:width, :],
                (((1,), (1,)), ((), ())),
                preferred_element_type=jnp.float32,
            )
            if mix_from is not None:
                acc[rows, :] = jnp.dot(
                    jnp.concatenate(weights, axis=1),
                    va[0:width, :],
                    preferred_element_type=jnp.float32,
                )
            query_pos = qp[rows, :]
            top = None
            for start in range(0, width, 128):
                seen = kp[0:1, start : start + 128] <= query_pos
                piece = jnp.where(seen, s[:, start : start + 128], HIDDEN)
                score_to[rows, start : start + 128] = piece
                top = piece if top is None else jnp.maximum(top, piece)
            mx[rows, :] = top

    def start_mix():
        top = jnp.max(mx[...], axis=1, keepdims=True) * SCALE
        tb[...] = jnp.broadcast_to(top, (ROWS, 128))

    def close_tile(tile):
        shift = lax.rem(own_x + NX - tile // OWN_TILES, NX)
        place = jnp.maximum(shift - 1, 0) * OWN_TILES + lax.rem(tile, OWN_TILES)
        total = acc[:, 128:256]
        result = acc[:, 0:128] / total
        spread = tb[...] + jnp.log2(total)
        stats = jnp.zeros((PART, 128), jnp.float32)
        for head in range(GROUP_HEADS):
            rows = slice(head * PART, (head + 1) * PART)
            out_ref[place, :, head * 128 : (head + 1) * 128] = result[rows].astype(jnp.bfloat16)
            level = spread[rows]
            high = level.astype(jnp.bfloat16).astype(jnp.float32)
            rest = level - high
            middle = rest.astype(jnp.bfloat16).astype(jnp.float32)
            low = rest - middle
            stats = jnp.where(lane == head, high, stats)
            stats = jnp.where(lane == 8 + head, middle, stats)
            stats = jnp.where(lane == 16 + head, low, stats)
        out_ref[place, :, WIDTH : WIDTH + 128] = stats.astype(jnp.bfloat16)

    first = meta[88 + first_place]
    open_tile(first)

    def run(score_to, mix_from, count):
        for number in range(1, KEYS // CHUNK + 1):
            pl.when(count == number)(functools.partial(both, score_to, mix_from, number))

    run(sc_even, None, meta[104 + first])
    start_mix()

    def two_tiles(pair, carry):
        for odd in range(2):
            k = pair * 2 + odd
            tile = meta[88 + first_place + k]
            following = meta[88 + first_place + jnp.minimum(k + 1, tiles - 1)]
            open_tile(following)
            mix_from, score_to = (sc_odd, sc_even) if odd else (sc_even, sc_odd)
            run(score_to, mix_from, meta[104 + tile])
            close_tile(tile)
            start_mix()
        return carry

    lax.fori_loop(0, tiles // 2, two_tiles, 0)
    for number, target in enumerate(out_refs):
        target[...] = out_ref[number * OWN_TILES : (number + 1) * OWN_TILES]


def attend(mine, meta, q, own, other, key_pos):
    tiles = OWN_TILES if mine else TILES - OWN_TILES
    first_place = TILES - OWN_TILES if mine else 0

    def kernel(*refs):
        attend_kernel(tiles, first_place, *refs)

    return pl.pallas_call(
        kernel,
        out_shape=[jax.ShapeDtypeStruct((OWN_TILES, PART, WIDTH + 128), jnp.bfloat16)]
        * (tiles // OWN_TILES),
        grid_spec=pltpu.PrefetchScalarGridSpec(
            num_scalar_prefetch=1,
            grid=(),
            in_specs=[pl.BlockSpec(memory_space=pltpu.VMEM)] * 4,
            out_specs=[pl.BlockSpec(memory_space=pltpu.VMEM)] * (tiles // OWN_TILES),
            scratch_shapes=[
                pltpu.VMEM((tiles, PART, WIDTH + 128), jnp.bfloat16),
                pltpu.VMEM((ROWS, 128), jnp.bfloat16),
                pltpu.VMEM((KEYS, 128), jnp.bfloat16),
                pltpu.VMEM((KEYS, 256), jnp.bfloat16),
                pltpu.VMEM((ROWS, 128), jnp.int32),
                pltpu.VMEM((ROWS, KEYS), jnp.float32),
                pltpu.VMEM((ROWS, KEYS), jnp.float32),
                pltpu.VMEM((ROWS, 128), jnp.float32),
                pltpu.VMEM((ROWS, 128), jnp.float32),
                pltpu.VMEM((ROWS, 256), jnp.float32),
            ],
        ),
        compiler_params=pltpu.CompilerParams(vmem_limit_bytes=48 * 1024 * 1024),
        name="attend_own" if mine else "attend_rest",
    )(meta, q, own, other, key_pos)


def merge_kernel(*refs):
    parts, out_ref = refs[:NX], refs[NX]
    levels = []
    for part in parts:
        stats = part[:, WIDTH : WIDTH + 128].astype(jnp.float32)
        levels.append((stats + pltpu.roll(stats, 120, 1)) + pltpu.roll(stats, 112, 1))
    top = levels[0]
    for level in levels[1:]:
        top = jnp.maximum(top, level)
    shares = [jnp.exp2(level - top) for level in levels]
    total = shares[0]
    for share in shares[1:]:
        total = total + share
    shares = [share / total for share in shares]
    for head in range(GROUP_HEADS):
        columns = slice(head * 128, (head + 1) * 128)
        mixed = sum(
            part[:, columns].astype(jnp.float32) * share[:, head : head + 1]
            for part, share in zip(parts, shares)
        )
        for z in range(NZ):
            out_ref[z, :, columns] = mixed[z * PIECE : (z + 1) * PIECE].astype(jnp.bfloat16)


def merge(parts):
    return pl.pallas_call(
        merge_kernel,
        out_shape=jax.ShapeDtypeStruct((NZ, PIECE, WIDTH), jnp.bfloat16),
        name="merge",
    )(*parts)


def pack_kernel(q_ref, k_ref, v_ref, out_ref):
    for z in range(NZ):
        out_ref[z, :, 0:WIDTH] = q_ref[:, z * WIDTH : (z + 1) * WIDTH]
        columns = slice(z * HEAD_DIMENSION, (z + 1) * HEAD_DIMENSION)
        out_ref[z, :, WIDTH : WIDTH + 128] = k_ref[:, columns]
        out_ref[z, :, WIDTH + 128 : WIDTH + 256] = v_ref[:, columns]


def pack(queries, keys, values):
    return pl.pallas_call(
        pack_kernel,
        out_shape=jax.ShapeDtypeStruct((NZ, PIECE, WIDTH + 256), jnp.bfloat16),
        name="pack",
    )(queries, keys, values)


def schedule(block_order):
    table = block_order.reshape(NZL, NX, NY, 2)
    key_block = lax.dynamic_index_in_dim(table, lax.axis_index("x"), 1, keepdims=False)
    key_block = key_block.transpose(1, 0, 2).reshape(NB)
    query_block = lax.dynamic_index_in_dim(table, lax.axis_index("y"), 2, keepdims=False)
    query_block = query_block.transpose(1, 0, 2).reshape(TILES)
    rank = jnp.sum((key_block[None, :] < key_block[:, None]).astype(jnp.int32), axis=1)
    numbers = jnp.arange(NB, dtype=jnp.int32)
    in_order = jnp.sum(
        jnp.where(rank[None, :] == numbers[:, None], key_block[None, :], 0), axis=1
    )
    seen = jnp.sum((key_block[None, :] <= query_block[:, None]).astype(jnp.int32), axis=1)
    chunks = jnp.maximum((seen * BLOCK_TOKENS + CHUNK - 1) // CHUNK, 1)
    tiles = jnp.arange(TILES, dtype=jnp.int32)
    own_x = lax.axis_index("x")
    remote = (tiles // OWN_TILES != own_x).astype(jnp.int32)
    weight = (remote * 64 + chunks) * TILES + tiles
    place = jnp.sum((weight[None, :] > weight[:, None]).astype(jnp.int32), axis=1)
    tile_at = jnp.sum(jnp.where(place[None, :] == tiles[:, None], tiles[None, :], 0), axis=1)
    spot = jnp.arange(BLOCK_TOKENS, dtype=jnp.int32)
    core = lax.axis_index("core")
    key_core = jnp.where(spot < PART, core, 1 - core)
    inner = spot % PART
    place = (inner // PIECE) * PART + inner % PIECE + key_core * PIECE
    key_pos = in_order[:, None] * BLOCK_TOKENS + place[None, :]
    head = jnp.concatenate([core.reshape(1), own_x.reshape(1), jnp.zeros((6,), jnp.int32)])
    meta = jnp.concatenate([head, rank, in_order, query_block, tile_at, chunks])
    return meta, key_pos.reshape(1, KEYS)


def ring(shift, size):
    return [(i, (i + shift) % size) for i in range(size)]


def over(x, axes):
    return lax.all_to_all(x, axes, split_axis=0, concat_axis=0, tiled=True)


def on_device(queries, keys, values, block_order):
    z_axes = ("zl", "zh")
    packed = pack(queries, keys, values)
    packed = over(packed, z_axes).reshape(TOKENS, WIDTH + 256)
    kv = packed[:, WIDTH:]
    q = over(jnp.broadcast_to(packed[None, :, :WIDTH], (NX, TOKENS, WIDTH)), "x")
    own = lax.all_gather(kv, "y", axis=0, tiled=True)
    own = own.reshape(NB, PART, 256)
    other = lax.ppermute(own, "core", ring(1, 2))
    meta, key_pos = schedule(block_order)
    q = q.reshape(TILES, PART, WIDTH)
    shape = (TOKENS, WIDTH + 128)
    rest = attend(False, meta, q, own, other, key_pos)
    parts = [
        lax.ppermute(rest[shift - 1].reshape(shape), "x", ring(-shift, NX)) for shift in (2, 1, 3)
    ]
    mine = attend(True, meta, q, own, other, key_pos)
    parts.append(mine[0].reshape(shape))
    attended = over(merge(parts), z_axes)
    return attended.transpose(1, 0, 2).reshape(PIECE, NZ * WIDTH)


def solution(mesh):
    fine = Mesh(mesh.devices.reshape(NZL, NX, NY, NZH, 2), AXES)
    rows = P(AXES, None)
    return jax.shard_map(
        on_device, mesh=fine, in_specs=(rows, rows, rows, P()), out_specs=rows, check_vma=False
    )
```

```python
import functools

import jax
import jax.numpy as jnp
from jax import lax
from jax.experimental import pallas as pl
from jax.experimental.pallas import tpu as pltpu
from jax.sharding import Mesh, PartitionSpec as P


HEAD_DIMENSION = 128
GROUP_HEADS = 8
PIECE = 20
BLOCK_TOKENS = 80
NX, NY, NZL, NZH = 4, 8, 2, 4
NZ = NZL * NZH
AXES = ("zl", "x", "y", "zh", "core")
LOG2E = 1.4426950408889634
SCALE = HEAD_DIMENSION ** (-0.5) * LOG2E
HIDDEN = -1e30
NB = NZL * NY * 2
KEYS = NB * BLOCK_TOKENS
TOKENS = NZ * PIECE
WIDTH = GROUP_HEADS * HEAD_DIMENSION
PART = 2 * PIECE
OWN_TILES = NZL * 2
TILES = NX * OWN_TILES
ROWS = GROUP_HEADS * PART
CHUNK = 512
STRIP = 160


def attend_kernel(
    tiles, first_place, meta, q_ref, own_ref, other_ref, kp, *refs
):
    out_refs = refs[: tiles // OWN_TILES]
    out_ref, qa, ka, va, qp, sc_even, sc_odd, mx, tb, acc = refs[tiles // OWN_TILES :]
    core = meta[0]
    own_x = meta[1]

    def load_block(block, carry):
        rank = meta[8 + block]
        both = jnp.concatenate(
            [own_ref[block].astype(jnp.float32), other_ref[block].astype(jnp.float32)], axis=0
        ).astype(jnp.bfloat16)
        start = pl.multiple_of(rank * BLOCK_TOKENS, 16)
        ka[pl.ds(start, BLOCK_TOKENS), :] = both[:, 0:128]
        va[pl.ds(start, BLOCK_TOKENS), 0:128] = both[:, 128:256]
        return carry

    lax.fori_loop(0, NB, load_block, 0, unroll=4)
    va[:, 128:256] = jnp.ones((KEYS, 128), jnp.bfloat16)
    row = lax.broadcasted_iota(jnp.int32, (PART, 128), 0)
    row_offset = (row // PIECE) * PART + row % PIECE + core * PIECE
    lane = lax.broadcasted_iota(jnp.int32, (PART, 128), 1)

    def open_tile(tile):
        heads = [
            q_ref[tile, :, head * 128 : (head + 1) * 128].astype(jnp.float32)
            for head in range(GROUP_HEADS)
        ]
        qa[...] = jnp.concatenate(heads, axis=0).astype(jnp.bfloat16)
        pos = row_offset + meta[72 + tile] * BLOCK_TOKENS
        qp[...] = jnp.concatenate([pos] * GROUP_HEADS, axis=0)

    def both(score_to, mix_from, count):
        width = count * CHUNK
        for at in range(0, ROWS, STRIP):
            rows = slice(at, at + STRIP)
            if mix_from is not None:
                level = tb[rows, :]
                weights = [
                    jnp.exp2(mix_from[rows, start : start + 128] * SCALE - level).astype(
                        jnp.bfloat16
                    )
                    for start in range(0, width, 128)
                ]
            s = lax.dot_general(
                qa[rows, :],
                ka[0:width, :],
                (((1,), (1,)), ((), ())),
                preferred_element_type=jnp.float32,
            )
            if mix_from is not None:
                acc[rows, :] = jnp.dot(
                    jnp.concatenate(weights, axis=1),
                    va[0:width, :],
                    preferred_element_type=jnp.float32,
                )
            query_pos = qp[rows, :]
            top = None
            for start in range(0, width, 128):
                seen = kp[0:1, start : start + 128] <= query_pos
                piece = jnp.where(seen, s[:, start : start + 128], HIDDEN)
                score_to[rows, start : start + 128] = piece
                top = piece if top is None else jnp.maximum(top, piece)
            mx[rows, :] = top

    def start_mix():
        top = jnp.max(mx[...], axis=1, keepdims=True) * SCALE
        tb[...] = jnp.broadcast_to(top, (ROWS, 128))

    def close_tile(tile):
        shift = lax.rem(own_x + NX - tile // OWN_TILES, NX)
        place = lax.rem(tile, OWN_TILES)
        if tiles > OWN_TILES:
            place += (shift // 2) * OWN_TILES
        total = acc[:, 128:256]
        result = acc[:, 0:128] / total
        spread = tb[...] + jnp.log2(total)
        stats = jnp.zeros((PART, 128), jnp.float32)
        for head in range(GROUP_HEADS):
            rows = slice(head * PART, (head + 1) * PART)
            out_ref[place, :, head * 128 : (head + 1) * 128] = result[rows].astype(jnp.bfloat16)
            level = spread[rows]
            high = level.astype(jnp.bfloat16).astype(jnp.float32)
            rest = level - high
            middle = rest.astype(jnp.bfloat16).astype(jnp.float32)
            low = rest - middle
            stats = jnp.where(lane == head, high, stats)
            stats = jnp.where(lane == 8 + head, middle, stats)
            stats = jnp.where(lane == 16 + head, low, stats)
        out_ref[place, :, WIDTH : WIDTH + 128] = stats.astype(jnp.bfloat16)

    first = meta[88 + first_place]
    open_tile(first)

    def run(score_to, mix_from, count):
        for number in range(1, KEYS // CHUNK + 1):
            pl.when(count == number)(functools.partial(both, score_to, mix_from, number))

    both(sc_even, None, KEYS // CHUNK)
    start_mix()

    def two_tiles(pair, carry):
        for odd in range(2):
            k = pair * 2 + odd
            tile = meta[88 + first_place + k]
            following = meta[88 + first_place + jnp.minimum(k + 1, tiles - 1)]
            open_tile(following)
            mix_from, score_to = (sc_odd, sc_even) if odd else (sc_even, sc_odd)
            run(score_to, mix_from, meta[104 + tile])
            close_tile(tile)
            start_mix()
        return carry

    lax.fori_loop(0, tiles // 2, two_tiles, 0)
    for number, target in enumerate(out_refs):
        target[...] = out_ref[number * OWN_TILES : (number + 1) * OWN_TILES]


def attend(first_place, tiles, meta, q, own, other, key_pos):
    def kernel(*refs):
        attend_kernel(tiles, first_place, *refs)

    return pl.pallas_call(
        kernel,
        out_shape=[jax.ShapeDtypeStruct((OWN_TILES, PART, WIDTH + 128), jnp.bfloat16)]
        * (tiles // OWN_TILES),
        grid_spec=pltpu.PrefetchScalarGridSpec(
            num_scalar_prefetch=1,
            grid=(),
            in_specs=[pl.BlockSpec(memory_space=pltpu.VMEM)] * 4,
            out_specs=[pl.BlockSpec(memory_space=pltpu.VMEM)] * (tiles // OWN_TILES),
            scratch_shapes=[
                pltpu.VMEM((tiles, PART, WIDTH + 128), jnp.bfloat16),
                pltpu.VMEM((ROWS, 128), jnp.bfloat16),
                pltpu.VMEM((KEYS, 128), jnp.bfloat16),
                pltpu.VMEM((KEYS, 256), jnp.bfloat16),
                pltpu.VMEM((ROWS, 128), jnp.int32),
                pltpu.VMEM((ROWS, KEYS), jnp.float32),
                pltpu.VMEM((ROWS, KEYS), jnp.float32),
                pltpu.VMEM((ROWS, 128), jnp.float32),
                pltpu.VMEM((ROWS, 128), jnp.float32),
                pltpu.VMEM((ROWS, 256), jnp.float32),
            ],
        ),
        compiler_params=pltpu.CompilerParams(vmem_limit_bytes=48 * 1024 * 1024),
    )(meta, q, own, other, key_pos)


def merge_kernel(*refs):
    parts, out_ref = refs[:NX], refs[NX]
    levels = []
    for part in parts:
        stats = part[:, WIDTH : WIDTH + 128].astype(jnp.float32)
        levels.append((stats + pltpu.roll(stats, 120, 1)) + pltpu.roll(stats, 112, 1))
    top = levels[0]
    for level in levels[1:]:
        top = jnp.maximum(top, level)
    shares = [jnp.exp2(level - top) for level in levels]
    total = shares[0]
    for share in shares[1:]:
        total = total + share
    shares = [share / total for share in shares]
    for head in range(GROUP_HEADS):
        columns = slice(head * 128, (head + 1) * 128)
        mixed = sum(
            part[:, columns].astype(jnp.float32) * share[:, head : head + 1]
            for part, share in zip(parts, shares)
        )
        for z in range(NZ):
            out_ref[z, :, columns] = mixed[z * PIECE : (z + 1) * PIECE].astype(jnp.bfloat16)


def merge(parts):
    return pl.pallas_call(
        merge_kernel,
        out_shape=jax.ShapeDtypeStruct((NZ, PIECE, WIDTH), jnp.bfloat16),
        in_specs=[pl.BlockSpec(memory_space=pltpu.VMEM)] * NX,
        out_specs=pl.BlockSpec(memory_space=pltpu.VMEM),
        name="merge",
    )(*parts)


def pack_kernel(q_ref, k_ref, v_ref, out_ref):
    for z in range(NZ):
        out_ref[z, :, 0:WIDTH] = q_ref[:, z * WIDTH : (z + 1) * WIDTH]
        columns = slice(z * HEAD_DIMENSION, (z + 1) * HEAD_DIMENSION)
        out_ref[z, :, WIDTH : WIDTH + 128] = k_ref[:, columns]
        out_ref[z, :, WIDTH + 128 : WIDTH + 256] = v_ref[:, columns]


def pack(queries, keys, values):
    return pl.pallas_call(
        pack_kernel,
        out_shape=jax.ShapeDtypeStruct((NZ, PIECE, WIDTH + 256), jnp.bfloat16),
        name="pack",
    )(queries, keys, values)


def schedule(block_order):
    table = block_order.reshape(NZL, NX, NY, 2)
    key_block = lax.dynamic_index_in_dim(table, lax.axis_index("x"), 1, keepdims=False)
    key_block = key_block.transpose(1, 0, 2).reshape(NB)
    query_block = lax.dynamic_index_in_dim(table, lax.axis_index("y"), 2, keepdims=False)
    query_block = query_block.transpose(1, 0, 2).reshape(TILES)
    rank = jnp.sum((key_block[None, :] < key_block[:, None]).astype(jnp.int32), axis=1)
    numbers = jnp.arange(NB, dtype=jnp.int32)
    in_order = jnp.sum(
        jnp.where(rank[None, :] == numbers[:, None], key_block[None, :], 0), axis=1
    )
    seen = jnp.sum((key_block[None, :] <= query_block[:, None]).astype(jnp.int32), axis=1)
    chunks = jnp.maximum((seen * BLOCK_TOKENS + CHUNK - 1) // CHUNK, 1)
    tiles = jnp.arange(TILES, dtype=jnp.int32)
    own_x = lax.axis_index("x")
    shift = (own_x + NX - tiles // OWN_TILES) % NX
    turn = jnp.where(shift == 2, 2, jnp.where(shift == 0, 0, 1))
    weight = (turn * 64 + chunks) * TILES + tiles
    place = jnp.sum((weight[None, :] > weight[:, None]).astype(jnp.int32), axis=1)
    tile_at = jnp.sum(jnp.where(place[None, :] == tiles[:, None], tiles[None, :], 0), axis=1)
    spot = jnp.arange(BLOCK_TOKENS, dtype=jnp.int32)
    core = lax.axis_index("core")
    key_core = jnp.where(spot < PART, core, 1 - core)
    inner = spot % PART
    place = (inner // PIECE) * PART + inner % PIECE + key_core * PIECE
    key_pos = in_order[:, None] * BLOCK_TOKENS + place[None, :]
    head = jnp.concatenate([core.reshape(1), own_x.reshape(1), jnp.zeros((6,), jnp.int32)])
    meta = jnp.concatenate([head, rank, in_order, query_block, tile_at, chunks])
    return meta, key_pos.reshape(1, KEYS)


def ring(shift, size):
    return [(i, (i + shift) % size) for i in range(size)]


def over(x, axes):
    return lax.all_to_all(x, axes, split_axis=0, concat_axis=0, tiled=True)


def on_device(queries, keys, values, block_order):
    z_axes = ("zl", "zh")
    packed = pack(queries, keys, values)
    packed = over(packed, z_axes).reshape(TOKENS, WIDTH + 256)
    kv = packed[:, WIDTH:]
    q = over(jnp.broadcast_to(packed[None, :, :WIDTH], (NX, TOKENS, WIDTH)), "x")
    own = lax.all_gather(kv, "y", axis=0, tiled=True)
    own = own.reshape(NB, PART, 256)
    other = lax.ppermute(own, "core", ring(1, 2))
    meta, key_pos = schedule(block_order)
    q = q.reshape(TILES, PART, WIDTH)
    shape = (TOKENS, WIDTH + 128)
    inputs = (meta, q, own, other, key_pos)

    def send(part, shift):
        return lax.ppermute(part.reshape(shape), "x", ring(-shift, NX))

    far = attend(0, OWN_TILES, *inputs)
    parts = [send(far[0], 2)]
    near = attend(OWN_TILES, 2 * OWN_TILES, *inputs)
    parts += [send(near[0], 1), send(near[1], 3)]
    mine = attend(3 * OWN_TILES, OWN_TILES, *inputs)
    parts.append(mine[0].reshape(shape))
    attended = over(merge(parts), z_axes)
    return attended.transpose(1, 0, 2).reshape(PIECE, NZ * WIDTH)


def solution(mesh):
    fine = Mesh(mesh.devices.reshape(NZL, NX, NY, NZH, 2), AXES)
    rows = P(AXES, None)
    return jax.shard_map(
        on_device, mesh=fine, in_specs=(rows, rows, rows, P()), out_specs=rows, check_vma=False
    )
```

```python
import functools

import jax
import jax.numpy as jnp
from jax import lax
from jax.experimental import pallas as pl
from jax.experimental.pallas import tpu as pltpu
from jax.sharding import Mesh, PartitionSpec as P


HEAD_DIMENSION = 128
GROUP_HEADS = 8
PIECE = 20
BLOCK_TOKENS = 80
NX, NY, NZL, NZH = 4, 8, 2, 4
NZ = NZL * NZH
AXES = ("zl", "x", "y", "zh", "core")
LOG2E = 1.4426950408889634
SCALE = HEAD_DIMENSION ** (-0.5) * LOG2E
HIDDEN = -1e30
NB = NZL * NY * 2
KEYS = NB * BLOCK_TOKENS
TOKENS = NZ * PIECE
WIDTH = GROUP_HEADS * HEAD_DIMENSION
PART = 2 * PIECE
OWN_TILES = NZL * 2
TILES = NX * OWN_TILES
ROWS = GROUP_HEADS * PART
CHUNK = 512
STRIP = 160


def attend_kernel(
    tiles, first_place, meta, q_ref, own_ref, other_ref, kp, *refs
):
    out_refs = refs[: tiles // OWN_TILES]
    out_ref, qa, ka, va, qp, sc_even, sc_odd, mx, tb, acc = refs[tiles // OWN_TILES :]
    core = meta[0]
    own_x = meta[1]

    def load_block(block, carry):
        rank = meta[8 + block]
        both = jnp.concatenate(
            [own_ref[block].astype(jnp.float32), other_ref[block].astype(jnp.float32)], axis=0
        ).astype(jnp.bfloat16)
        start = pl.multiple_of(rank * BLOCK_TOKENS, 16)
        ka[pl.ds(start, BLOCK_TOKENS), :] = both[:, 0:128]
        va[pl.ds(start, BLOCK_TOKENS), 0:128] = both[:, 128:256]
        return carry

    lax.fori_loop(0, NB, load_block, 0, unroll=4)
    va[:, 128:256] = jnp.ones((KEYS, 128), jnp.bfloat16)
    row = lax.broadcasted_iota(jnp.int32, (PART, 128), 0)
    row_offset = (row // PIECE) * PART + row % PIECE + core * PIECE
    lane = lax.broadcasted_iota(jnp.int32, (PART, 128), 1)

    def open_tile(tile):
        heads = [
            q_ref[tile, :, head * 128 : (head + 1) * 128].astype(jnp.float32)
            for head in range(GROUP_HEADS)
        ]
        qa[...] = jnp.concatenate(heads, axis=0).astype(jnp.bfloat16)
        pos = row_offset + meta[72 + tile] * BLOCK_TOKENS
        qp[...] = pos

    def both(score_to, mix_from, count):
        width = count * CHUNK
        for at in range(0, ROWS, STRIP):
            rows = slice(at, at + STRIP)
            if mix_from is not None:
                level = tb[rows, :]
                weights = [
                    jnp.exp2(mix_from[rows, start : start + 128] * SCALE - level).astype(
                        jnp.bfloat16
                    )
                    for start in range(0, width, 128)
                ]
            s = lax.dot_general(
                qa[rows, :],
                ka[0:width, :],
                (((1,), (1,)), ((), ())),
                preferred_element_type=jnp.float32,
            )
            if mix_from is not None:
                acc[rows, :] = jnp.dot(
                    jnp.concatenate(weights, axis=1),
                    va[0:width, :],
                    preferred_element_type=jnp.float32,
                )
            query_pos = jnp.concatenate([qp[...]] * (STRIP // PART), axis=0)
            top = None
            for start in range(0, width, 128):
                seen = kp[0:1, start : start + 128] <= query_pos
                piece = jnp.where(seen, s[:, start : start + 128], HIDDEN)
                score_to[rows, start : start + 128] = piece
                top = piece if top is None else jnp.maximum(top, piece)
            mx[rows, :] = top

    def start_mix():
        top = jnp.max(mx[...], axis=1, keepdims=True) * SCALE
        tb[...] = jnp.broadcast_to(top, (ROWS, 128))

    def close_tile(tile):
        shift = lax.rem(own_x + NX - tile // OWN_TILES, NX)
        place = lax.rem(tile, OWN_TILES)
        if tiles > OWN_TILES:
            place += (shift // 2) * OWN_TILES
        total = acc[:, 128:256]
        result = acc[:, 0:128] / total
        top = tb[...]
        level_top = jnp.zeros((PART, 128), jnp.float32)
        level_total = jnp.ones((PART, 128), jnp.float32)
        for head in range(GROUP_HEADS):
            rows = slice(head * PART, (head + 1) * PART)
            out_ref[place, :, head * 128 : (head + 1) * 128] = result[rows].astype(jnp.bfloat16)
            level_top = jnp.where(lane == head, top[rows], level_top)
            level_total = jnp.where(lane == head, total[rows], level_total)
        level = level_top + jnp.log2(level_total)
        high = level.astype(jnp.bfloat16).astype(jnp.float32)
        rest = level - high
        middle = rest.astype(jnp.bfloat16).astype(jnp.float32)
        low = rest - middle
        stats = (high + pltpu.roll(middle, 8, 1)) + pltpu.roll(low, 16, 1)
        out_ref[place, :, WIDTH : WIDTH + 128] = stats.astype(jnp.bfloat16)

    first = meta[88 + first_place]
    open_tile(first)

    def run(score_to, mix_from, count):
        for number in range(1, KEYS // CHUNK + 1):
            pl.when(count == number)(functools.partial(both, score_to, mix_from, number))

    both(sc_even, None, KEYS // CHUNK)
    start_mix()

    def two_tiles(pair, carry):
        for odd in range(2):
            k = pair * 2 + odd
            tile = meta[88 + first_place + k]
            following = meta[88 + first_place + jnp.minimum(k + 1, tiles - 1)]
            open_tile(following)
            mix_from, score_to = (sc_odd, sc_even) if odd else (sc_even, sc_odd)
            run(score_to, mix_from, meta[104 + tile])
            close_tile(tile)
            start_mix()
        return carry

    lax.fori_loop(0, tiles // 2, two_tiles, 0)
    for number, target in enumerate(out_refs):
        target[...] = out_ref[number * OWN_TILES : (number + 1) * OWN_TILES]


def attend(first_place, tiles, meta, q, own, other, key_pos):
    def kernel(*refs):
        attend_kernel(tiles, first_place, *refs)

    return pl.pallas_call(
        kernel,
        out_shape=[jax.ShapeDtypeStruct((OWN_TILES, PART, WIDTH + 128), jnp.bfloat16)]
        * (tiles // OWN_TILES),
        grid_spec=pltpu.PrefetchScalarGridSpec(
            num_scalar_prefetch=1,
            grid=(),
            in_specs=[pl.BlockSpec(memory_space=pltpu.VMEM)] * 4,
            out_specs=[pl.BlockSpec(memory_space=pltpu.VMEM)] * (tiles // OWN_TILES),
            scratch_shapes=[
                pltpu.VMEM((tiles, PART, WIDTH + 128), jnp.bfloat16),
                pltpu.VMEM((ROWS, 128), jnp.bfloat16),
                pltpu.VMEM((KEYS, 128), jnp.bfloat16),
                pltpu.VMEM((KEYS, 256), jnp.bfloat16),
                pltpu.VMEM((PART, 128), jnp.int32),
                pltpu.VMEM((ROWS, KEYS), jnp.float32),
                pltpu.VMEM((ROWS, KEYS), jnp.float32),
                pltpu.VMEM((ROWS, 128), jnp.float32),
                pltpu.VMEM((ROWS, 128), jnp.float32),
                pltpu.VMEM((ROWS, 256), jnp.float32),
            ],
        ),
        compiler_params=pltpu.CompilerParams(vmem_limit_bytes=48 * 1024 * 1024),
    )(meta, q, own, other, key_pos)


def merge_kernel(*refs):
    parts, out_ref = refs[:NX], refs[NX]
    levels = []
    for part in parts:
        stats = part[:, WIDTH : WIDTH + 128].astype(jnp.float32)
        levels.append((stats + pltpu.roll(stats, 120, 1)) + pltpu.roll(stats, 112, 1))
    top = levels[0]
    for level in levels[1:]:
        top = jnp.maximum(top, level)
    shares = [jnp.exp2(level - top) for level in levels]
    total = shares[0]
    for share in shares[1:]:
        total = total + share
    row = lax.broadcasted_iota(jnp.int32, (256, WIDTH), 0)
    column = lax.broadcasted_iota(jnp.int32, (256, WIDTH), 1)
    lift = jnp.where(row % 128 == column // 128, 1.0, 0.0).astype(jnp.bfloat16)
    mixed = None
    for part, share in zip(parts, shares):
        share = share / total
        high = share.astype(jnp.bfloat16)
        low = (share - high.astype(jnp.float32)).astype(jnp.bfloat16)
        wide = jnp.dot(
            jnp.concatenate([high, low], axis=1), lift, preferred_element_type=jnp.float32
        )
        term = part[:, 0:WIDTH].astype(jnp.float32) * wide
        mixed = term if mixed is None else mixed + term
    for z in range(NZ):
        out_ref[z] = mixed[z * PIECE : (z + 1) * PIECE].astype(jnp.bfloat16)


def merge(parts):
    return pl.pallas_call(
        merge_kernel,
        out_shape=jax.ShapeDtypeStruct((NZ, PIECE, WIDTH), jnp.bfloat16),
        in_specs=[pl.BlockSpec(memory_space=pltpu.VMEM)] * NX,
        out_specs=pl.BlockSpec(memory_space=pltpu.VMEM),
        name="merge",
    )(*parts)


def pack_kernel(q_ref, k_ref, v_ref, out_ref):
    for z in range(NZ):
        out_ref[z, :, 0:WIDTH] = q_ref[:, z * WIDTH : (z + 1) * WIDTH]
        columns = slice(z * HEAD_DIMENSION, (z + 1) * HEAD_DIMENSION)
        out_ref[z, :, WIDTH : WIDTH + 128] = k_ref[:, columns]
        out_ref[z, :, WIDTH + 128 : WIDTH + 256] = v_ref[:, columns]


def pack(queries, keys, values):
    return pl.pallas_call(
        pack_kernel,
        out_shape=jax.ShapeDtypeStruct((NZ, PIECE, WIDTH + 256), jnp.bfloat16),
        name="pack",
    )(queries, keys, values)


def schedule(block_order):
    table = block_order.reshape(NZL, NX, NY, 2)
    key_block = lax.dynamic_index_in_dim(table, lax.axis_index("x"), 1, keepdims=False)
    key_block = key_block.transpose(1, 0, 2).reshape(NB)
    query_block = lax.dynamic_index_in_dim(table, lax.axis_index("y"), 2, keepdims=False)
    query_block = query_block.transpose(1, 0, 2).reshape(TILES)
    rank = jnp.sum((key_block[None, :] < key_block[:, None]).astype(jnp.int32), axis=1)
    numbers = jnp.arange(NB, dtype=jnp.int32)
    in_order = jnp.sum(
        jnp.where(rank[None, :] == numbers[:, None], key_block[None, :], 0), axis=1
    )
    seen = jnp.sum((key_block[None, :] <= query_block[:, None]).astype(jnp.int32), axis=1)
    chunks = jnp.maximum((seen * BLOCK_TOKENS + CHUNK - 1) // CHUNK, 1)
    tiles = jnp.arange(TILES, dtype=jnp.int32)
    own_x = lax.axis_index("x")
    shift = (own_x + NX - tiles // OWN_TILES) % NX
    turn = jnp.where(shift == 2, 2, jnp.where(shift == 0, 0, 1))
    weight = (turn * 64 + chunks) * TILES + tiles
    place = jnp.sum((weight[None, :] > weight[:, None]).astype(jnp.int32), axis=1)
    tile_at = jnp.sum(jnp.where(place[None, :] == tiles[:, None], tiles[None, :], 0), axis=1)
    spot = jnp.arange(BLOCK_TOKENS, dtype=jnp.int32)
    core = lax.axis_index("core")
    key_core = jnp.where(spot < PART, core, 1 - core)
    inner = spot % PART
    place = (inner // PIECE) * PART + inner % PIECE + key_core * PIECE
    key_pos = in_order[:, None] * BLOCK_TOKENS + place[None, :]
    head = jnp.concatenate([core.reshape(1), own_x.reshape(1), jnp.zeros((6,), jnp.int32)])
    meta = jnp.concatenate([head, rank, in_order, query_block, tile_at, chunks])
    return meta, key_pos.reshape(1, KEYS)


def ring(shift, size):
    return [(i, (i + shift) % size) for i in range(size)]


def over(x, axes):
    return lax.all_to_all(x, axes, split_axis=0, concat_axis=0, tiled=True)


def on_device(queries, keys, values, block_order):
    z_axes = ("zl", "zh")
    packed = pack(queries, keys, values)
    packed = over(packed, z_axes).reshape(TOKENS, WIDTH + 256)
    kv = packed[:, WIDTH:]
    q = over(jnp.broadcast_to(packed[None, :, :WIDTH], (NX, TOKENS, WIDTH)), "x")
    own = lax.all_gather(kv, "y", axis=0, tiled=True)
    own = own.reshape(NB, PART, 256)
    other = lax.ppermute(own, "core", ring(1, 2))
    meta, key_pos = schedule(block_order)
    q = q.reshape(TILES, PART, WIDTH)
    shape = (TOKENS, WIDTH + 128)
    inputs = (meta, q, own, other, key_pos)

    def send(part, shift):
        return lax.ppermute(part.reshape(shape), "x", ring(-shift, NX))

    far = attend(0, OWN_TILES, *inputs)
    parts = [send(far[0], 2)]
    near = attend(OWN_TILES, 2 * OWN_TILES, *inputs)
    parts += [send(near[0], 1), send(near[1], 3)]
    mine = attend(3 * OWN_TILES, OWN_TILES, *inputs)
    parts.append(mine[0].reshape(shape))
    attended = over(merge(parts), z_axes)
    return attended.transpose(1, 0, 2).reshape(PIECE, NZ * WIDTH)


def solution(mesh):
    fine = Mesh(mesh.devices.reshape(NZL, NX, NY, NZH, 2), AXES)
    rows = P(AXES, None)
    return jax.shard_map(
        on_device, mesh=fine, in_specs=(rows, rows, rows, P()), out_specs=rows, check_vma=False
    )
```

```python
import functools

import jax
import jax.numpy as jnp
from jax import lax
from jax.experimental import pallas as pl
from jax.experimental.pallas import tpu as pltpu
from jax.sharding import Mesh, PartitionSpec as P


HEAD_DIMENSION = 128
GROUP_HEADS = 8
PIECE = 20
BLOCK_TOKENS = 80
NX, NY, NZL, NZH = 4, 8, 2, 4
NZ = NZL * NZH
AXES = ("zl", "x", "y", "zh", "core")
LOG2E = 1.4426950408889634
SCALE = HEAD_DIMENSION ** (-0.5) * LOG2E
HIDDEN = -1e30
NB = NZL * NY * 2
KEYS = NB * BLOCK_TOKENS
TOKENS = NZ * PIECE
WIDTH = GROUP_HEADS * HEAD_DIMENSION
PART = 2 * PIECE
OWN_TILES = NZL * 2
TILES = NX * OWN_TILES
ROWS = GROUP_HEADS * PART
CHUNK = 512
STRIP = 160


def attend_kernel(
    tiles, first_place, meta, q_ref, own_ref, other_ref, kp, *refs
):
    out_refs = refs[: tiles // OWN_TILES]
    refs = refs[tiles // OWN_TILES :]
    if first_place == 0:
        ka, va, *refs = refs
    else:
        ka, va = own_ref, other_ref
    out_ref, qa, qp, sc_even, sc_odd, mx, tb, acc = refs
    core = meta[0]
    own_x = meta[1]

    def load_block(block, carry):
        rank = meta[8 + block]
        both = jnp.concatenate(
            [own_ref[block].astype(jnp.float32), other_ref[block].astype(jnp.float32)], axis=0
        ).astype(jnp.bfloat16)
        start = pl.multiple_of(rank * BLOCK_TOKENS, 16)
        ka[pl.ds(start, BLOCK_TOKENS), :] = both[:, 0:128]
        va[pl.ds(start, BLOCK_TOKENS), 0:128] = both[:, 128:256]
        return carry

    if first_place == 0:
        lax.fori_loop(0, NB, load_block, 0, unroll=4)
        va[:, 128:256] = jnp.ones((KEYS, 128), jnp.bfloat16)
    row = lax.broadcasted_iota(jnp.int32, (PART, 128), 0)
    row_offset = (row // PIECE) * PART + row % PIECE + core * PIECE
    lane = lax.broadcasted_iota(jnp.int32, (PART, 128), 1)

    def open_tile(tile):
        heads = [
            q_ref[tile, :, head * 128 : (head + 1) * 128].astype(jnp.float32)
            for head in range(GROUP_HEADS)
        ]
        qa[...] = jnp.concatenate(heads, axis=0).astype(jnp.bfloat16)
        pos = row_offset + meta[72 + tile] * BLOCK_TOKENS
        qp[...] = pos

    def both(score_to, mix_from, count):
        width = count * CHUNK
        for at in range(0, ROWS, STRIP):
            rows = slice(at, at + STRIP)
            if mix_from is not None:
                level = tb[rows, :]
                weights = [
                    jnp.exp2(mix_from[rows, start : start + 128] * SCALE - level).astype(
                        jnp.bfloat16
                    )
                    for start in range(0, width, 128)
                ]
            s = lax.dot_general(
                qa[rows, :],
                ka[0:width, :],
                (((1,), (1,)), ((), ())),
                preferred_element_type=jnp.float32,
            )
            if mix_from is not None:
                acc[rows, :] = jnp.dot(
                    jnp.concatenate(weights, axis=1),
                    va[0:width, :],
                    preferred_element_type=jnp.float32,
                )
            query_pos = jnp.concatenate([qp[...]] * (STRIP // PART), axis=0)
            top = None
            for start in range(0, width, 128):
                seen = kp[0:1, start : start + 128] <= query_pos
                piece = jnp.where(seen, s[:, start : start + 128], HIDDEN)
                score_to[rows, start : start + 128] = piece
                top = piece if top is None else jnp.maximum(top, piece)
            mx[rows, :] = top

    def start_mix():
        top = jnp.max(mx[...], axis=1, keepdims=True) * SCALE
        tb[...] = jnp.broadcast_to(top, (ROWS, 128))

    def close_tile(tile):
        shift = lax.rem(own_x + NX - tile // OWN_TILES, NX)
        place = lax.rem(tile, OWN_TILES)
        if tiles > OWN_TILES:
            place += (shift // 2) * OWN_TILES
        total = acc[:, 128:256]
        result = acc[:, 0:128] / total
        top = tb[...]
        level_top = jnp.zeros((PART, 128), jnp.float32)
        level_total = jnp.ones((PART, 128), jnp.float32)
        for head in range(GROUP_HEADS):
            rows = slice(head * PART, (head + 1) * PART)
            out_ref[place, :, head * 128 : (head + 1) * 128] = result[rows].astype(jnp.bfloat16)
            level_top = jnp.where(lane == head, top[rows], level_top)
            level_total = jnp.where(lane == head, total[rows], level_total)
        level = level_top + jnp.log2(level_total)
        high = level.astype(jnp.bfloat16).astype(jnp.float32)
        rest = level - high
        middle = rest.astype(jnp.bfloat16).astype(jnp.float32)
        low = rest - middle
        stats = (high + pltpu.roll(middle, 8, 1)) + pltpu.roll(low, 16, 1)
        out_ref[place, :, WIDTH : WIDTH + 128] = stats.astype(jnp.bfloat16)

    first = meta[88 + first_place]
    open_tile(first)

    def run(score_to, mix_from, count):
        for number in range(1, KEYS // CHUNK + 1):
            pl.when(count == number)(functools.partial(both, score_to, mix_from, number))

    both(sc_even, None, KEYS // CHUNK)
    start_mix()

    def two_tiles(pair, carry):
        for odd in range(2):
            k = pair * 2 + odd
            tile = meta[88 + first_place + k]
            following = meta[88 + first_place + jnp.minimum(k + 1, tiles - 1)]
            open_tile(following)
            mix_from, score_to = (sc_odd, sc_even) if odd else (sc_even, sc_odd)
            run(score_to, mix_from, meta[104 + tile])
            close_tile(tile)
            start_mix()
        return carry

    lax.fori_loop(0, tiles // 2, two_tiles, 0)
    for number, target in enumerate(out_refs):
        target[...] = out_ref[number * OWN_TILES : (number + 1) * OWN_TILES]


def attend(first_place, tiles, meta, q, own, other, key_pos):
    part = jax.ShapeDtypeStruct((OWN_TILES, PART, WIDTH + 128), jnp.bfloat16)
    shapes = [part] * (tiles // OWN_TILES)
    if first_place == 0:
        shapes += [jax.ShapeDtypeStruct((KEYS, width), jnp.bfloat16) for width in (128, 256)]

    def kernel(*refs):
        attend_kernel(tiles, first_place, *refs)

    return pl.pallas_call(
        kernel,
        out_shape=shapes,
        grid_spec=pltpu.PrefetchScalarGridSpec(
            num_scalar_prefetch=1,
            grid=(),
            in_specs=[pl.BlockSpec(memory_space=pltpu.VMEM)] * 4,
            out_specs=[pl.BlockSpec(memory_space=pltpu.VMEM)] * len(shapes),
            scratch_shapes=[
                pltpu.VMEM((tiles, PART, WIDTH + 128), jnp.bfloat16),
                pltpu.VMEM((ROWS, 128), jnp.bfloat16),
                pltpu.VMEM((PART, 128), jnp.int32),
                pltpu.VMEM((ROWS, KEYS), jnp.float32),
                pltpu.VMEM((ROWS, KEYS), jnp.float32),
                pltpu.VMEM((ROWS, 128), jnp.float32),
                pltpu.VMEM((ROWS, 128), jnp.float32),
                pltpu.VMEM((ROWS, 256), jnp.float32),
            ],
        ),
        compiler_params=pltpu.CompilerParams(vmem_limit_bytes=48 * 1024 * 1024),
    )(meta, q, own, other, key_pos)


def merge_kernel(*refs):
    parts, out_ref = refs[:NX], refs[NX]
    levels = []
    for part in parts:
        stats = part[:, WIDTH : WIDTH + 128].astype(jnp.float32)
        levels.append((stats + pltpu.roll(stats, 120, 1)) + pltpu.roll(stats, 112, 1))
    top = levels[0]
    for level in levels[1:]:
        top = jnp.maximum(top, level)
    shares = [jnp.exp2(level - top) for level in levels]
    total = shares[0]
    for share in shares[1:]:
        total = total + share
    row = lax.broadcasted_iota(jnp.int32, (256, WIDTH), 0)
    column = lax.broadcasted_iota(jnp.int32, (256, WIDTH), 1)
    lift = jnp.where(row % 128 == column // 128, 1.0, 0.0).astype(jnp.bfloat16)
    mixed = None
    for part, share in zip(parts, shares):
        share = share / total
        high = share.astype(jnp.bfloat16)
        low = (share - high.astype(jnp.float32)).astype(jnp.bfloat16)
        wide = jnp.dot(
            jnp.concatenate([high, low], axis=1), lift, preferred_element_type=jnp.float32
        )
        term = part[:, 0:WIDTH].astype(jnp.float32) * wide
        mixed = term if mixed is None else mixed + term
    for z in range(NZ):
        out_ref[z] = mixed[z * PIECE : (z + 1) * PIECE].astype(jnp.bfloat16)


def merge(parts):
    return pl.pallas_call(
        merge_kernel,
        out_shape=jax.ShapeDtypeStruct((NZ, PIECE, WIDTH), jnp.bfloat16),
        in_specs=[pl.BlockSpec(memory_space=pltpu.VMEM)] * NX,
        out_specs=pl.BlockSpec(memory_space=pltpu.VMEM),
        name="merge",
    )(*parts)


def pack_kernel(q_ref, k_ref, v_ref, out_ref):
    for z in range(NZ):
        out_ref[z, :, 0:WIDTH] = q_ref[:, z * WIDTH : (z + 1) * WIDTH]
        columns = slice(z * HEAD_DIMENSION, (z + 1) * HEAD_DIMENSION)
        out_ref[z, :, WIDTH : WIDTH + 128] = k_ref[:, columns]
        out_ref[z, :, WIDTH + 128 : WIDTH + 256] = v_ref[:, columns]


def pack(queries, keys, values):
    return pl.pallas_call(
        pack_kernel,
        out_shape=jax.ShapeDtypeStruct((NZ, PIECE, WIDTH + 256), jnp.bfloat16),
        name="pack",
    )(queries, keys, values)


def schedule(block_order):
    table = block_order.reshape(NZL, NX, NY, 2)
    key_block = lax.dynamic_index_in_dim(table, lax.axis_index("x"), 1, keepdims=False)
    key_block = key_block.transpose(1, 0, 2).reshape(NB)
    query_block = lax.dynamic_index_in_dim(table, lax.axis_index("y"), 2, keepdims=False)
    query_block = query_block.transpose(1, 0, 2).reshape(TILES)
    rank = jnp.sum((key_block[None, :] < key_block[:, None]).astype(jnp.int32), axis=1)
    numbers = jnp.arange(NB, dtype=jnp.int32)
    in_order = jnp.sum(
        jnp.where(rank[None, :] == numbers[:, None], key_block[None, :], 0), axis=1
    )
    seen = jnp.sum((key_block[None, :] <= query_block[:, None]).astype(jnp.int32), axis=1)
    chunks = jnp.maximum((seen * BLOCK_TOKENS + CHUNK - 1) // CHUNK, 1)
    tiles = jnp.arange(TILES, dtype=jnp.int32)
    own_x = lax.axis_index("x")
    shift = (own_x + NX - tiles // OWN_TILES) % NX
    turn = jnp.where(shift == 2, 2, jnp.where(shift == 0, 0, 1))
    weight = (turn * 64 + chunks) * TILES + tiles
    place = jnp.sum((weight[None, :] > weight[:, None]).astype(jnp.int32), axis=1)
    tile_at = jnp.sum(jnp.where(place[None, :] == tiles[:, None], tiles[None, :], 0), axis=1)
    spot = jnp.arange(BLOCK_TOKENS, dtype=jnp.int32)
    core = lax.axis_index("core")
    key_core = jnp.where(spot < PART, core, 1 - core)
    inner = spot % PART
    place = (inner // PIECE) * PART + inner % PIECE + key_core * PIECE
    key_pos = in_order[:, None] * BLOCK_TOKENS + place[None, :]
    head = jnp.concatenate([core.reshape(1), own_x.reshape(1), jnp.zeros((6,), jnp.int32)])
    meta = jnp.concatenate([head, rank, in_order, query_block, tile_at, chunks])
    return meta, key_pos.reshape(1, KEYS)


def ring(shift, size):
    return [(i, (i + shift) % size) for i in range(size)]


def over(x, axes):
    return lax.all_to_all(x, axes, split_axis=0, concat_axis=0, tiled=True)


def on_device(queries, keys, values, block_order):
    z_axes = ("zl", "zh")
    packed = pack(queries, keys, values)
    packed = over(packed, z_axes).reshape(TOKENS, WIDTH + 256)
    kv = packed[:, WIDTH:]
    q = over(jnp.broadcast_to(packed[None, :, :WIDTH], (NX, TOKENS, WIDTH)), "x")
    own = lax.all_gather(kv, "y", axis=0, tiled=True)
    own = own.reshape(NB, PART, 256)
    other = lax.ppermute(own, "core", ring(1, 2))
    meta, key_pos = schedule(block_order)
    q = q.reshape(TILES, PART, WIDTH)
    shape = (TOKENS, WIDTH + 128)

    def send(part, shift):
        return lax.ppermute(part.reshape(shape), "x", ring(-shift, NX))

    far = attend(0, OWN_TILES, meta, q, own, other, key_pos)
    inputs = (meta, q, far[1], far[2], key_pos)
    parts = [send(far[0], 2)]
    near = attend(OWN_TILES, 2 * OWN_TILES, *inputs)
    parts += [send(near[0], 1), send(near[1], 3)]
    mine = attend(3 * OWN_TILES, OWN_TILES, *inputs)
    parts.append(mine[0].reshape(shape))
    attended = over(merge(parts), z_axes)
    return attended.transpose(1, 0, 2).reshape(PIECE, NZ * WIDTH)


def solution(mesh):
    fine = Mesh(mesh.devices.reshape(NZL, NX, NY, NZH, 2), AXES)
    rows = P(AXES, None)
    return jax.shard_map(
        on_device, mesh=fine, in_specs=(rows, rows, rows, P()), out_specs=rows, check_vma=False
    )
```
